256 devices in a mesh: wide: 32 (over z, y_lo, core), narrow: 8 (over x, y_hi).
Axes of the slice: x: 4, y: 4 (y_hi: 2, y_lo: 2; y = y_hi * 2 + y_lo), z: 8, core: 2. Of those that a mesh axis runs over, the one named last changes fastest.
Arguments:
- gradient: bfloat16 [40960, 16384], P(('wide', 'narrow')), may hold values from -81 to 81
- seating: int32 [64], replicated, may hold values from 0 to 63, each once
Outputs:
- rotated: bfloat16 [40960, 16384], P(('wide', 'narrow'))
The draws below stay inside these ranges and needn't reach their ends.
Inputs may be any that keep to these rules, and one draw needn't show every extreme that they name: `seating`: each of the 64 block numbers is the seat of exactly one block.
All inputs are finite; a program needn't handle non-finite values.
Results may differ from the reference program's by a relative error of at most 0.0075.
Values may be sent and summed in bfloat16 or wider, within the bound.
A program may use at most 64 MiB of HBM per device.

```python
import math
import jax
import jax.numpy as jnp
from jax import lax

BW = 256
ROWS = 40960
ROUNDS = 8
STEPS = 2
BLOCKS = 64
COLS = 16384


def draw_gradient(key, part):
    keys = jax.random.split(key, 3)
    row_scale = jnp.exp(jax.random.uniform(keys[0], (ROWS, 1), jnp.float32, math.log(0.3), math.log(3.0)))
    col_scale = jnp.exp(jax.random.uniform(keys[1], (1, COLS), jnp.float32, math.log(0.3), math.log(3.0)))
    noise = jnp.clip(jax.random.normal(keys[2], (ROWS, COLS), jnp.float32), -5.0, 5.0)
    values = noise * row_scale * col_scale
    return values.astype(jnp.bfloat16)


def setup_inputs(seed: int = 0) -> dict:
    key_list = jax.random.split(jax.random.key(seed), 3)
    return {
        "gradient": draw_gradient(jax.random.fold_in(key_list[2], 71), 0),
        "seating": jax.random.permutation(key_list[1], BLOCKS).astype(jnp.int32),
    }


def advance(seat_of, total_slots):
    pair_count = total_slots // 2
    cycle_pos = jnp.where(seat_of % 2 == 0, seat_of // 2 - 1, total_slots - 2 - (seat_of - 1) // 2)
    next_pos = (cycle_pos + 1) % (total_slots - 1)
    new_slot = jnp.where(next_pos < pair_count - 1, 2 * (next_pos + 1), 2 * (total_slots - 2 - next_pos) + 1)
    return jnp.where(seat_of == 0, 0, new_slot).astype(jnp.int32)

def occupants(seat_of, total_slots):
    block_ids = jnp.arange(total_slots, dtype=jnp.int32)
    matches = seat_of[None, :] == block_ids[:, None]
    return lax.optimization_barrier(jnp.sum(jnp.where(matches, block_ids[None, :], 0), axis=1)).astype(jnp.int32)

def rotate_columns(matrix, cosine, sine_part):
    width = cosine.shape[0]
    left_cols = matrix[:, :width]
    right_cols = matrix[:, width:]
    return jnp.concatenate([left_cols * cosine - right_cols * sine_part, left_cols * sine_part + right_cols * cosine], axis=1)

def roll_second(matrix, offset, which_axis):
    head_part, tail_part = jnp.split(matrix, 2, axis=which_axis)
    return jnp.concatenate([head_part, jnp.roll(tail_part, offset, axis=which_axis)], axis=which_axis)

def one_round(round_index, carried):
    gram_mat, rotation = carried
    width = gram_mat.shape[0] // 2
    left_diag = jnp.diagonal(gram_mat[:width, :width])
    right_diag = jnp.diagonal(gram_mat[width:, width:])
    off_diag = jnp.diagonal(gram_mat[:width, width:])
    spread = right_diag - left_diag
    damping = (left_diag + right_diag) / 16.0 + 1e-06
    radius = jnp.sqrt(spread * spread + 4.0 * off_diag * off_diag + damping * damping)
    tangent = 2.0 * off_diag / (spread + radius)
    cosine = 1.0 / jnp.sqrt(1.0 + tangent * tangent)
    sine_part = tangent * cosine
    gram_mat = rotate_columns(gram_mat, cosine, sine_part)
    gram_mat = rotate_columns(gram_mat.T, cosine, sine_part).T
    rotation = rotate_columns(rotation, cosine, sine_part)
    gram_mat = roll_second(roll_second(gram_mat, -1, 0), -1, 1)
    rotation = roll_second(rotation, -1, 1)
    return (gram_mat, rotation)

def rotations(gram_mat):
    initial = (gram_mat, jnp.eye(gram_mat.shape[0], dtype=jnp.float32))
    gram_mat, rotation = lax.fori_loop(0, ROUNDS, one_round, initial)
    return roll_second(rotation, ROUNDS, 1)

def update_pair(pair_data):
    gram_mat = jnp.dot(pair_data.T, pair_data, preferred_element_type=jnp.float32)
    rotation = rotations(gram_mat).astype(jnp.bfloat16)
    return jnp.dot(pair_data, rotation, preferred_element_type=jnp.float32).astype(jnp.bfloat16)

def reference(gradient, seating):
    blocks_all = gradient.reshape(ROWS, BLOCKS, BW)
    seat_of = seating.astype(jnp.int32)
    for section_index in range(STEPS):
        if section_index > 0:
            seat_of = advance(seat_of, BLOCKS)
        holders = occupants(seat_of, BLOCKS)
        seated = jnp.take(blocks_all, holders, axis=1)
        pair_data = seated.reshape(ROWS, BLOCKS // 2, 2 * BW).transpose(1, 0, 2)
        new_pairs = lax.map(update_pair, pair_data)
        seated = new_pairs.transpose(1, 0, 2).reshape(ROWS, BLOCKS, BW)
        blocks_all = jnp.take(seated, seat_of, axis=1)
    return blocks_all.reshape(ROWS, COLS)
```

```python
import functools

import jax
import jax.numpy as jnp
from jax import lax
from jax.experimental import pallas as pl
from jax.experimental.pallas import tpu as pltpu
from jax.sharding import PartitionSpec as P

ROUNDS = 8
BW = 256
F32 = jnp.float32
BF16 = jnp.bfloat16


def advance(seat_of, total_slots):
    pair_count = total_slots // 2
    cycle_pos = jnp.where(seat_of % 2 == 0, seat_of // 2 - 1, total_slots - 2 - (seat_of - 1) // 2)
    next_pos = (cycle_pos + 1) % (total_slots - 1)
    new_slot = jnp.where(
        next_pos < pair_count - 1, 2 * (next_pos + 1), 2 * (total_slots - 2 - next_pos) + 1
    )
    return jnp.where(seat_of == 0, 0, new_slot)


def occupants(seat_of, total_slots):
    block_ids = jnp.arange(total_slots, dtype=jnp.int32)
    matches = seat_of[None, :] == block_ids[:, None]
    return jnp.sum(jnp.where(matches, block_ids[None, :], 0), axis=1).astype(jnp.int32)


def init_masks(mask_ref):
    s = lax.broadcasted_iota(jnp.int32, (8, 128), 0)
    c = lax.broadcasted_iota(jnp.int32, (8, 128), 1)
    for t in range(-1, 17):
        d = 8 * t + s - c
        mask_ref[t + 1] = jnp.where((d >= -7) & (d <= 7), 1.0, 0.0).astype(F32)
    for t in range(17):
        d = 8 * t + s - c
        mask_ref[18 + t] = jnp.where((d >= 0) & (d <= 7), 1.0, 0.0).astype(F32)


def dot_t(a, b):
    return lax.dot_general(a, b, (((0,), (0,)), ((), ())), preferred_element_type=F32)


def gram_band(left, right, mask_ref, g_ref, store):
    g_ref[0] = dot_t(left, right)
    g_ref[1] = dot_t(left, left)
    g_ref[2] = dot_t(right, right)
    for j in range(2):
        lanes = slice(128 * j, 128 * j + 128)
        acc = [jnp.zeros((8, 128), F32) for _ in range(4)]
        for t in range(-1, 17):
            u = (16 * j + t) % 32
            acc[u % 2] += g_ref[0, 8 * u : 8 * u + 8, lanes] * mask_ref[t + 1]
        for t in range(17):
            u = (16 * j + t) % 32
            mask = mask_ref[18 + t]
            acc[2 + u % 2] += g_ref[1, 8 * u : 8 * u + 8, lanes] * mask
            acc[2 + (u + 1) % 2] += g_ref[2, 8 * u : 8 * u + 8, lanes] * mask
        for r in range(4):
            store(slice(8 * r, 8 * r + 8), lanes, acc[r])


def lane_roll(x, back):
    return pltpu.roll(x, (-back) % x.shape[1], 1)


def row_roll(x, down):
    return pltpu.roll(x, down % x.shape[0], 0)


def iota(shape, axis):
    return lax.broadcasted_iota(jnp.int32, shape, axis)


def skew(x, sign):
    c = iota(x.shape, 1)
    for b in (1, 2, 4, 8):
        x = jnp.where((c & b) != 0, row_roll(x, sign * b), x)
    return x


def spread(x):
    y = jnp.broadcast_to(x, (8, x.shape[1]))
    d = iota(y.shape, 0)
    for b in (1, 2, 4):
        y = jnp.where((d & b) != 0, lane_roll(y, b), y)
    return y


def rotation_band(band):
    cross = skew(band[:16], -1)
    own = skew(band[16:], -1)
    lr = cross[:8]
    ll = own[:8]
    rr = own[8:]
    d = iota((8, BW), 0)
    flipped = [lr[0:1]] + [lane_roll(cross[16 - k : 17 - k], k) for k in range(1, 8)]
    rl = jnp.concatenate(flipped, axis=0)
    ca = jnp.where(d == 0, 1.0, 0.0).astype(F32)
    cb = jnp.zeros((8, BW), F32)
    cc = jnp.zeros((8, BW), F32)
    cd = ca
    for r in range(ROUNDS):
        a = ll[0:1]
        c = rr[0:1]
        off = lr[0:1]
        spread_ac = c - a
        damp = (a + c) / 16.0 + 1e-06
        radius = jnp.sqrt(spread_ac * spread_ac + 4.0 * off * off + damp * damp)
        tangent = 2.0 * off / (spread_ac + radius)
        cs = 1.0 / jnp.sqrt(1.0 + tangent * tangent)
        sn = tangent * cs
        if r < ROUNDS - 1:
            csd = spread(cs)
            snd = spread(sn)
            ll1 = ll * cs - lr * sn
            lr1 = ll * sn + lr * cs
            rl1 = rl * cs - rr * sn
            rr1 = rl * sn + rr * cs
            ll = csd * ll1 - snd * rl1
            rl = snd * ll1 + csd * rl1
            lr = csd * lr1 - snd * rr1
            rr = snd * lr1 + csd * rr1
        ca, cc = cs * ca - sn * cc, sn * ca + cs * cc
        cb, cd = cs * cb - sn * cd, sn * cb + cs * cd
        if r < ROUNDS - 1:
            lr = jnp.where(d == 0, row_roll(rl, -1), row_roll(lane_roll(lr, 1), 1))
            rl = jnp.where(d == 7, 0.0, row_roll(rl, -1))
            rr = lane_roll(rr, 1)
            cc = jnp.where(d == 0, 0.0, row_roll(lane_roll(cc, 1), 1))
            cd = jnp.where(d == 0, 0.0, row_roll(lane_roll(cd, 1), 1))
    first = jnp.concatenate([ca, cb], axis=0)
    second = row_roll(jnp.concatenate([lane_roll(cd, -7), lane_roll(cc, -7)], axis=0), 1)
    return jnp.concatenate([skew(first, 1), skew(second, 1)], axis=0)


def build_dense(rot, m_ref):
    wide = rot.astype(F32)
    s = iota((16, 128), 0)
    c = iota((16, 128), 1)
    for half in range(2):
        part = wide[16 * half : 16 * half + 16]
        turned = jnp.concatenate([part[8:], part[:8]], axis=0)
        for j in range(2):
            lanes = slice(128 * j, 128 * j + 128)
            out_lanes = slice(256 * half + 128 * j, 256 * half + 128 * j + 128)
            for g in (range(0, 9) if half == 0 else range(-1, 8)):
                d = 16 * g + s - c
                keep = ((d >= 0) & (d <= 7)) if half == 0 else ((d >= -7) & (d <= 0))
                row = 16 * ((g + 8 * j) % 16)
                m_ref[row : row + 16, out_lanes] = jnp.where(keep, part[:, lanes], 0.0).astype(BF16)
                m_ref[256 + row : 256 + row + 16, out_lanes] = jnp.where(
                    keep, turned[:, lanes], 0.0
                ).astype(BF16)


def apply_dense(left, right, m_ref):
    new = jnp.dot(left, m_ref[:256], preferred_element_type=F32)
    return (new + jnp.dot(right, m_ref[256:], preferred_element_type=F32)).astype(BF16)


def gram_kernel(hold, l_ref, r_ref, out_ref, mask_ref, g_ref):
    @pl.when(pl.program_id(0) == 0)
    def _():
        init_masks(mask_ref)

    def store(rows, lanes, value):
        out_ref[0, rows, lanes] = value

    gram_band(l_ref[...], r_ref[...], mask_ref, g_ref, store)


def previous_seats(q, pairs):
    left = jnp.where(q == 0, 0, jnp.where(q == 1, 1, 2 * q - 2))
    right = jnp.where(q == pairs - 1, 2 * pairs - 2, 2 * q + 3)
    return left, right


def middle_kernel(pairs, hold, l_ref, r_ref, rot_ref, x_ref, out_ref, mask_ref, g_ref, m_ref):
    p = pl.program_id(0)

    @pl.when(p == 0)
    def _():
        init_masks(mask_ref)
        m_ref[...] = jnp.zeros_like(m_ref)

    @pl.when(p < pairs)
    def _():
        build_dense(rot_ref[0], m_ref)
        cols = pl.ds(pl.multiple_of(p * 2 * BW, 2 * BW), 2 * BW)
        x_ref[:, cols] = apply_dense(l_ref[...], r_ref[...], m_ref)

    @pl.when(p >= 1)
    def _():
        def store(rows, lanes, value):
            out_ref[0, rows, lanes] = value

        left, right = previous_seats(p - 1, pairs)
        l_new = x_ref[:, pl.ds(pl.multiple_of(left * BW, BW), BW)]
        r_new = x_ref[:, pl.ds(pl.multiple_of(right * BW, BW), BW)]
        gram_band(l_new, r_new, mask_ref, g_ref, store)


def last_kernel(pairs, hold, l_ref, r_ref, rot_ref, out_ref, m_ref, y_ref):
    q = pl.program_id(0)
    side = pl.program_id(1)

    @pl.when((q == 0) & (side == 0))
    def _():
        m_ref[...] = jnp.zeros_like(m_ref)

    @pl.when(side == 0)
    def _():
        build_dense(rot_ref[0], m_ref)
        new = apply_dense(l_ref[...], r_ref[...], m_ref)
        out_ref[...] = new[:, :BW]
        y_ref[...] = new[:, BW:]

    @pl.when(side == 1)
    def _():
        out_ref[...] = y_ref[...]


def gram_call(x, holders, pairs):
    rows = x.shape[0]
    return pl.pallas_call(
        gram_kernel,
        out_shape=jax.ShapeDtypeStruct((pairs, 32, BW), F32),
        grid_spec=pltpu.PrefetchScalarGridSpec(
            num_scalar_prefetch=1,
            grid=(pairs,),
            in_specs=[
                pl.BlockSpec((rows, BW), lambda p, h: (0, h[2 * p])),
                pl.BlockSpec((rows, BW), lambda p, h: (0, h[2 * p + 1])),
            ],
            out_specs=pl.BlockSpec((1, 32, BW), lambda p, h: (p, 0, 0)),
            scratch_shapes=[pltpu.VMEM((35, 8, 128), F32), pltpu.VMEM((3, BW, BW), F32)],
        ),
    )(holders, x, x)


def middle_call(x, holders, rot, pairs):
    rows, cols = x.shape
    last = pairs - 1
    return pl.pallas_call(
        functools.partial(middle_kernel, pairs),
        out_shape=(
            jax.ShapeDtypeStruct((rows, cols), BF16),
            jax.ShapeDtypeStruct((pairs, 32, BW), F32),
        ),
        grid_spec=pltpu.PrefetchScalarGridSpec(
            num_scalar_prefetch=1,
            grid=(pairs + 1,),
            in_specs=[
                pl.BlockSpec((rows, BW), lambda p, h: (0, h[2 * jnp.minimum(p, last)])),
                pl.BlockSpec((rows, BW), lambda p, h: (0, h[2 * jnp.minimum(p, last) + 1])),
                pl.BlockSpec((1, 32, BW), lambda p, h: (jnp.minimum(p, last), 0, 0)),
            ],
            out_specs=(
                pl.BlockSpec((rows, cols), lambda p, h: (0, 0)),
                pl.BlockSpec((1, 32, BW), lambda p, h: (jnp.maximum(p - 1, 0), 0, 0)),
            ),
            scratch_shapes=[
                pltpu.VMEM((35, 8, 128), F32),
                pltpu.VMEM((3, BW, BW), F32),
                pltpu.VMEM((2 * BW, 2 * BW), BF16),
            ],
        ),
    )(holders, x, x, rot)


def last_call(x, holders, rot, pairs):
    rows, cols = x.shape
    return pl.pallas_call(
        functools.partial(last_kernel, pairs),
        out_shape=jax.ShapeDtypeStruct((rows, cols), BF16),
        grid_spec=pltpu.PrefetchScalarGridSpec(
            num_scalar_prefetch=1,
            grid=(pairs, 2),
            in_specs=[
                pl.BlockSpec((rows, BW), lambda q, s, h: (0, previous_seats(q, pairs)[0])),
                pl.BlockSpec((rows, BW), lambda q, s, h: (0, previous_seats(q, pairs)[1])),
                pl.BlockSpec((1, 32, BW), lambda q, s, h: (q, 0, 0)),
            ],
            out_specs=pl.BlockSpec((rows, BW), lambda q, s, h: (0, h[2 * q + s])),
            scratch_shapes=[pltpu.VMEM((2 * BW, 2 * BW), BF16), pltpu.VMEM((rows, BW), BF16)],
        ),
    )(holders, x, x, rot)


def rounds_call(band):
    def kernel(in_ref, out_ref):
        out_ref[...] = rotation_band(in_ref[...]).astype(BF16)

    return pl.pallas_call(kernel, out_shape=jax.ShapeDtypeStruct((32, BW), BF16))(band)


def exchange(band, pairs):
    total = lax.psum(band, ("wide", "narrow"))
    mine = lax.dynamic_index_in_dim(total, lax.axis_index("wide"), 0, keepdims=False)
    return lax.all_gather(rounds_call(mine), "wide", axis=0, tiled=False)


def per_device(gradient, seating):
    slots = gradient.shape[1] // BW
    pairs = slots // 2
    seat_of = seating.astype(jnp.int32)
    first = occupants(seat_of, slots)
    second = occupants(advance(seat_of, slots), slots)
    rot = exchange(gram_call(gradient, first, pairs), pairs)
    moved, band = middle_call(gradient, first, rot, pairs)
    rot = exchange(band, pairs)
    return last_call(moved, second, rot, pairs)


def solution(mesh):
    in_specs = (P(("wide", "narrow"), None), P())
    out_specs = P(("wide", "narrow"), None)
    return jax.shard_map(
        per_device, mesh=mesh, in_specs=in_specs, out_specs=out_specs, check_vma=False
    )
```

```python
import functools

import jax
import jax.numpy as jnp
from jax import lax
from jax.experimental import pallas as pl
from jax.experimental.pallas import tpu as pltpu
from jax.sharding import PartitionSpec as P

ROUNDS = 8
BW = 256
F32 = jnp.float32
BF16 = jnp.bfloat16


def advance(seat_of, total_slots):
    pair_count = total_slots // 2
    cycle_pos = jnp.where(seat_of % 2 == 0, seat_of // 2 - 1, total_slots - 2 - (seat_of - 1) // 2)
    next_pos = (cycle_pos + 1) % (total_slots - 1)
    new_slot = jnp.where(
        next_pos < pair_count - 1, 2 * (next_pos + 1), 2 * (total_slots - 2 - next_pos) + 1
    )
    return jnp.where(seat_of == 0, 0, new_slot)


def occupants(seat_of, total_slots):
    block_ids = jnp.arange(total_slots, dtype=jnp.int32)
    matches = seat_of[None, :] == block_ids[:, None]
    return jnp.sum(jnp.where(matches, block_ids[None, :], 0), axis=1).astype(jnp.int32)


def init_masks(mask_ref):
    s = lax.broadcasted_iota(jnp.int32, (8, 128), 0)
    c = lax.broadcasted_iota(jnp.int32, (8, 128), 1)
    for t in range(-1, 17):
        d = 8 * t + s - c
        mask_ref[t + 1] = jnp.where((d >= -7) & (d <= 7), 1.0, 0.0).astype(F32)
    for t in range(17):
        d = 8 * t + s - c
        mask_ref[18 + t] = jnp.where((d >= 0) & (d <= 7), 1.0, 0.0).astype(F32)


def dot_t(a, b):
    return lax.dot_general(a, b, (((0,), (0,)), ((), ())), preferred_element_type=F32)


def gram_band(left, right, mask_ref, g_ref, store):
    g_ref[0] = dot_t(left, right)
    g_ref[1] = dot_t(left, left)
    g_ref[2] = dot_t(right, right)
    for j in range(2):
        lanes = slice(128 * j, 128 * j + 128)
        acc = [jnp.zeros((8, 128), F32) for _ in range(4)]
        for t in range(-1, 17):
            u = (16 * j + t) % 32
            acc[u % 2] += g_ref[0, 8 * u : 8 * u + 8, lanes] * mask_ref[t + 1]
        for t in range(17):
            u = (16 * j + t) % 32
            mask = mask_ref[18 + t]
            acc[2 + u % 2] += g_ref[1, 8 * u : 8 * u + 8, lanes] * mask
            acc[2 + (u + 1) % 2] += g_ref[2, 8 * u : 8 * u + 8, lanes] * mask
        for r in range(4):
            store(slice(8 * r, 8 * r + 8), lanes, acc[r])


def lane_roll(x, back):
    return pltpu.roll(x, (-back) % x.shape[1], 1)


def row_roll(x, down):
    return pltpu.roll(x, down % x.shape[0], 0)


def iota(shape, axis):
    return lax.broadcasted_iota(jnp.int32, shape, axis)


def skew(x, sign):
    c = iota(x.shape, 1)
    for b in (1, 2, 4, 8):
        x = jnp.where((c & b) != 0, row_roll(x, sign * b), x)
    return x


def spread(x):
    y = jnp.broadcast_to(x, (8, x.shape[1]))
    d = iota(y.shape, 0)
    for b in (1, 2, 4):
        y = jnp.where((d & b) != 0, lane_roll(y, b), y)
    return y


def rotation_band(band):
    cross = skew(band[:16], -1)
    own = skew(band[16:], -1)
    lr = cross[:8]
    ll = own[:8]
    rr = own[8:]
    d = iota((8, BW), 0)
    flipped = [lr[0:1]] + [lane_roll(cross[16 - k : 17 - k], k) for k in range(1, 8)]
    rl = jnp.concatenate(flipped, axis=0)
    ca = jnp.where(d == 0, 1.0, 0.0).astype(F32)
    cb = jnp.zeros((8, BW), F32)
    cc = jnp.zeros((8, BW), F32)
    cd = ca
    for r in range(ROUNDS):
        a = ll[0:1]
        c = rr[0:1]
        off = lr[0:1]
        spread_ac = c - a
        damp = (a + c) / 16.0 + 1e-06
        radius = jnp.sqrt(spread_ac * spread_ac + 4.0 * off * off + damp * damp)
        tangent = 2.0 * off / (spread_ac + radius)
        cs = 1.0 / jnp.sqrt(1.0 + tangent * tangent)
        sn = tangent * cs
        if r < ROUNDS - 1:
            csd = spread(cs)
            snd = spread(sn)
            ll1 = ll * cs - lr * sn
            lr1 = ll * sn + lr * cs
            rl1 = rl * cs - rr * sn
            rr1 = rl * sn + rr * cs
            ll = csd * ll1 - snd * rl1
            rl = snd * ll1 + csd * rl1
            lr = csd * lr1 - snd * rr1
            rr = snd * lr1 + csd * rr1
        ca, cc = cs * ca - sn * cc, sn * ca + cs * cc
        cb, cd = cs * cb - sn * cd, sn * cb + cs * cd
        if r < ROUNDS - 1:
            lr = jnp.where(d == 0, row_roll(rl, -1), row_roll(lane_roll(lr, 1), 1))
            rl = jnp.where(d == 7, 0.0, row_roll(rl, -1))
            rr = lane_roll(rr, 1)
            cc = jnp.where(d == 0, 0.0, row_roll(lane_roll(cc, 1), 1))
            cd = jnp.where(d == 0, 0.0, row_roll(lane_roll(cd, 1), 1))
    first = jnp.concatenate([ca, cb], axis=0)
    second = row_roll(jnp.concatenate([lane_roll(cd, -7), lane_roll(cc, -7)], axis=0), 1)
    return jnp.concatenate([skew(first, 1), skew(second, 1)], axis=0)


def build_dense(rot, m_ref):
    wide = rot.astype(F32)
    s = iota((16, 128), 0)
    c = iota((16, 128), 1)
    for half in range(2):
        part = wide[16 * half : 16 * half + 16]
        turned = jnp.concatenate([part[8:], part[:8]], axis=0)
        for j in range(2):
            lanes = slice(128 * j, 128 * j + 128)
            out_lanes = slice(256 * half + 128 * j, 256 * half + 128 * j + 128)
            for g in (range(0, 9) if half == 0 else range(-1, 8)):
                d = 16 * g + s - c
                keep = ((d >= 0) & (d <= 7)) if half == 0 else ((d >= -7) & (d <= 0))
                row = 16 * ((g + 8 * j) % 16)
                m_ref[row : row + 16, out_lanes] = jnp.where(keep, part[:, lanes], 0.0).astype(BF16)
                m_ref[256 + row : 256 + row + 16, out_lanes] = jnp.where(
                    keep, turned[:, lanes], 0.0
                ).astype(BF16)


def apply_dense(left, right, m_ref):
    new = jnp.dot(left, m_ref[:256], preferred_element_type=F32)
    return (new + jnp.dot(right, m_ref[256:], preferred_element_type=F32)).astype(BF16)


def gram_kernel(hold, l_ref, r_ref, out_ref, mask_ref, g_ref):
    @pl.when(pl.program_id(0) == 0)
    def _():
        init_masks(mask_ref)

    def store(rows, lanes, value):
        out_ref[0, rows, lanes] = value

    gram_band(l_ref[...], r_ref[...], mask_ref, g_ref, store)


def previous_seats(q, pairs):
    left = jnp.where(q == 0, 0, jnp.where(q == 1, 1, 2 * q - 2))
    right = jnp.where(q == pairs - 1, 2 * pairs - 2, 2 * q + 3)
    return left, right


def middle_kernel(pairs, hold, l_ref, r_ref, rot_ref, x_ref, out_ref, mask_ref, g_ref, m_ref):
    p = pl.program_id(0)

    @pl.when(p == 0)
    def _():
        init_masks(mask_ref)
        m_ref[...] = jnp.zeros_like(m_ref)

    @pl.when(p < pairs)
    def _():
        build_dense(rot_ref[0], m_ref)
        cols = pl.ds(pl.multiple_of(p * 2 * BW, 2 * BW), 2 * BW)
        x_ref[:, cols] = apply_dense(l_ref[...], r_ref[...], m_ref)

    @pl.when(p >= 1)
    def _():
        def store(rows, lanes, value):
            out_ref[0, rows, lanes] = value

        left, right = previous_seats(p - 1, pairs)
        l_new = x_ref[:, pl.ds(pl.multiple_of(left * BW, BW), BW)]
        r_new = x_ref[:, pl.ds(pl.multiple_of(right * BW, BW), BW)]
        gram_band(l_new, r_new, mask_ref, g_ref, store)


def last_kernel(pairs, hold, l_ref, r_ref, rot_ref, out_ref, m_ref, y_ref):
    q = pl.program_id(0)
    side = pl.program_id(1)

    @pl.when((q == 0) & (side == 0))
    def _():
        m_ref[...] = jnp.zeros_like(m_ref)

    @pl.when(side == 0)
    def _():
        build_dense(rot_ref[0], m_ref)
        new = apply_dense(l_ref[...], r_ref[...], m_ref)
        out_ref[...] = new[:, :BW]
        y_ref[...] = new[:, BW:]

    @pl.when(side == 1)
    def _():
        out_ref[...] = y_ref[...]


def gram_call(x, holders, pairs):
    rows = x.shape[0]
    return pl.pallas_call(
        gram_kernel,
        out_shape=jax.ShapeDtypeStruct((pairs, 32, BW), F32),
        grid_spec=pltpu.PrefetchScalarGridSpec(
            num_scalar_prefetch=1,
            grid=(pairs,),
            in_specs=[
                pl.BlockSpec((rows, BW), lambda p, h: (0, h[2 * p])),
                pl.BlockSpec((rows, BW), lambda p, h: (0, h[2 * p + 1])),
            ],
            out_specs=pl.BlockSpec((1, 32, BW), lambda p, h: (p, 0, 0)),
            scratch_shapes=[pltpu.VMEM((35, 8, 128), F32), pltpu.VMEM((3, BW, BW), F32)],
        ),
    )(holders, x, x)


def middle_call(x, holders, rot, pairs):
    rows, cols = x.shape
    last = pairs - 1
    return pl.pallas_call(
        functools.partial(middle_kernel, pairs),
        out_shape=(
            jax.ShapeDtypeStruct((rows, cols), BF16),
            jax.ShapeDtypeStruct((pairs, 32, BW), F32),
        ),
        grid_spec=pltpu.PrefetchScalarGridSpec(
            num_scalar_prefetch=1,
            grid=(pairs + 1,),
            in_specs=[
                pl.BlockSpec((rows, BW), lambda p, h: (0, h[2 * jnp.minimum(p, last)])),
                pl.BlockSpec((rows, BW), lambda p, h: (0, h[2 * jnp.minimum(p, last) + 1])),
                pl.BlockSpec((1, 32, BW), lambda p, h: (jnp.minimum(p, last), 0, 0)),
            ],
            out_specs=(
                pl.BlockSpec((rows, cols), lambda p, h: (0, 0)),
                pl.BlockSpec((1, 32, BW), lambda p, h: (jnp.maximum(p - 1, 0), 0, 0)),
            ),
            scratch_shapes=[
                pltpu.VMEM((35, 8, 128), F32),
                pltpu.VMEM((3, BW, BW), F32),
                pltpu.VMEM((2 * BW, 2 * BW), BF16),
            ],
        ),
    )(holders, x, x, rot)


def last_call(x, holders, rot, pairs):
    rows, cols = x.shape
    return pl.pallas_call(
        functools.partial(last_kernel, pairs),
        out_shape=jax.ShapeDtypeStruct((rows, cols), BF16),
        grid_spec=pltpu.PrefetchScalarGridSpec(
            num_scalar_prefetch=1,
            grid=(pairs, 2),
            in_specs=[
                pl.BlockSpec((rows, BW), lambda q, s, h: (0, previous_seats(q, pairs)[0])),
                pl.BlockSpec((rows, BW), lambda q, s, h: (0, previous_seats(q, pairs)[1])),
                pl.BlockSpec((1, 32, BW), lambda q, s, h: (q, 0, 0)),
            ],
            out_specs=pl.BlockSpec((rows, BW), lambda q, s, h: (0, h[2 * q + s])),
            scratch_shapes=[pltpu.VMEM((2 * BW, 2 * BW), BF16), pltpu.VMEM((rows, BW), BF16)],
        ),
    )(holders, x, x, rot)


def place():
    w = lax.axis_index("wide")
    n = lax.axis_index("narrow")
    z, y_lo, core = w // 4, (w // 2) % 2, w % 2
    x, y_hi = n // 2, n % 2
    return x, 2 * y_hi + y_lo, z, core


def device(x, y, z, core):
    return ((z * 2 + y % 2) * 2 + core, x * 2 + y // 2)


def exchange_kernel(
    in_ref, out_ref, r1, acc1, ra2, rb2, acca, accb, ra3, rb3, mine, rz, send_sem, recv_sem
):
    x, y, z, core = place()
    partner = device(x, y, z, 1 - core)
    along_x = [device((x + k) % 4, y, z, core) for k in range(1, 4)]
    along_y = [device(x, (y + k) % 4, z, core) for k in range(1, 4)]
    along_z = [device(x, y, (z + k) % 8, core) for k in range(1, 8)]

    barrier = pltpu.get_barrier_semaphore()
    greeted = [partner] + along_x + along_y + along_z
    for other in greeted:
        pl.semaphore_signal(barrier, inc=1, device_id=other, device_id_type=pl.DeviceIdType.MESH)
    pl.semaphore_wait(barrier, len(greeted))

    def remote(index, src, dst, target):
        return pltpu.make_async_remote_copy(
            src_ref=src,
            dst_ref=dst,
            send_sem=send_sem.at[index],
            recv_sem=recv_sem.at[index],
            device_id=target,
            device_id_type=pl.DeviceIdType.MESH,
        )

    def start(copies):
        for copy in copies:
            copy.start()

    def finish(copies):
        for copy in copies:
            copy.wait()

    swap = [remote(0, in_ref.at[1 - core], r1, partner)]
    start(swap)
    finish(swap)
    acc1[...] = in_ref[core] + r1[...]

    top, low = slice(0, 16), slice(16, 32)
    copies = []
    for k in range(1, 4):
        copies.append(remote(k, acc1.at[(x + k) % 4, :, top], ra2.at[k - 1], along_x[k - 1]))
        copies.append(remote(3 + k, acc1.at[:, (y + k) % 4, low], rb2.at[k - 1], along_y[k - 1]))
    start(copies)
    finish(copies)
    acca[...] = (acc1[x, :, top] + ra2[0]) + (ra2[1] + ra2[2])
    accb[...] = (acc1[:, y, low] + rb2[0]) + (rb2[1] + rb2[2])

    copies = []
    for k in range(1, 4):
        copies.append(remote(6 + k, acca.at[(y + k) % 4], ra3.at[k - 1], along_y[k - 1]))
        copies.append(remote(9 + k, accb.at[(x + k) % 4], rb3.at[k - 1], along_x[k - 1]))
    start(copies)
    finish(copies)
    mine[top] = (acca[y] + ra3[0]) + (ra3[1] + ra3[2])
    mine[low] = (accb[x] + rb3[0]) + (rb3[1] + rb3[2])

    copies = [remote(12 + k, mine, rz.at[z], along_z[k - 1]) for k in range(1, 8)]
    start(copies)
    rz[z] = mine[...]
    finish(copies)
    total = ((rz[0] + rz[1]) + (rz[2] + rz[3])) + ((rz[4] + rz[5]) + (rz[6] + rz[7]))

    out_ref[core, x, y] = rotation_band(total).astype(BF16)

    copies = []
    for k in range(1, 4):
        piece = out_ref.at[core, x, y, top]
        copies.append(remote(19 + k, piece, piece, along_y[k - 1]))
        piece = out_ref.at[core, x, y, low]
        copies.append(remote(22 + k, piece, piece, along_x[k - 1]))
    start(copies)
    finish(copies)
    copies = []
    for k in range(1, 4):
        piece = out_ref.at[core, x, :, top]
        copies.append(remote(25 + k, piece, piece, along_x[k - 1]))
        piece = out_ref.at[core, :, y, low]
        copies.append(remote(28 + k, piece, piece, along_y[k - 1]))
    start(copies)
    finish(copies)
    swap = [remote(32, out_ref.at[core], out_ref.at[core], partner)]
    start(swap)
    finish(swap)


def exchange(band, pairs):
    vmem = pl.BlockSpec(memory_space=pltpu.VMEM)
    out = pl.pallas_call(
        exchange_kernel,
        out_shape=jax.ShapeDtypeStruct((2, 4, 4, 32, BW), BF16),
        in_specs=[vmem],
        out_specs=vmem,
        scratch_shapes=[
            pltpu.VMEM((4, 4, 32, BW), F32),
            pltpu.VMEM((4, 4, 32, BW), F32),
            pltpu.VMEM((3, 4, 16, BW), F32),
            pltpu.VMEM((3, 4, 16, BW), F32),
            pltpu.VMEM((4, 16, BW), F32),
            pltpu.VMEM((4, 16, BW), F32),
            pltpu.VMEM((3, 16, BW), F32),
            pltpu.VMEM((3, 16, BW), F32),
            pltpu.VMEM((32, BW), F32),
            pltpu.VMEM((8, 32, BW), F32),
            pltpu.SemaphoreType.DMA((33,)),
            pltpu.SemaphoreType.DMA((33,)),
        ],
        compiler_params=pltpu.CompilerParams(collective_id=0, has_side_effects=True),
    )(band.reshape(2, 4, 4, 32, BW))
    return out.reshape(pairs, 32, BW)


def per_device(gradient, seating):
    slots = gradient.shape[1] // BW
    pairs = slots // 2
    seat_of = seating.astype(jnp.int32)
    first = occupants(seat_of, slots)
    second = occupants(advance(seat_of, slots), slots)
    rot = exchange(gram_call(gradient, first, pairs), pairs)
    moved, band = middle_call(gradient, first, rot, pairs)
    rot = exchange(band, pairs)
    return last_call(moved, second, rot, pairs)


def solution(mesh):
    in_specs = (P(("wide", "narrow"), None), P())
    out_specs = P(("wide", "narrow"), None)
    return jax.shard_map(
        per_device, mesh=mesh, in_specs=in_specs, out_specs=out_specs, check_vma=False
    )
```

```python
import functools

import jax
import jax.numpy as jnp
from jax import lax
from jax.experimental import pallas as pl
from jax.experimental.pallas import tpu as pltpu
from jax.sharding import PartitionSpec as P

ROUNDS = 8
BW = 256
F32 = jnp.float32
BF16 = jnp.bfloat16


def advance(seat_of, total_slots):
    pair_count = total_slots // 2
    cycle_pos = jnp.where(seat_of % 2 == 0, seat_of // 2 - 1, total_slots - 2 - (seat_of - 1) // 2)
    next_pos = (cycle_pos + 1) % (total_slots - 1)
    new_slot = jnp.where(
        next_pos < pair_count - 1, 2 * (next_pos + 1), 2 * (total_slots - 2 - next_pos) + 1
    )
    return jnp.where(seat_of == 0, 0, new_slot)


def occupants(seat_of, total_slots):
    block_ids = jnp.arange(total_slots, dtype=jnp.int32)
    matches = seat_of[None, :] == block_ids[:, None]
    return jnp.sum(jnp.where(matches, block_ids[None, :], 0), axis=1).astype(jnp.int32)


def init_masks(mask_ref):
    s = lax.broadcasted_iota(jnp.int32, (8, 128), 0)
    c = lax.broadcasted_iota(jnp.int32, (8, 128), 1)
    for t in range(-1, 17):
        d = 8 * t + s - c
        mask_ref[t + 1] = jnp.where((d >= -7) & (d <= 7), 1.0, 0.0).astype(F32)
    for t in range(17):
        d = 8 * t + s - c
        mask_ref[18 + t] = jnp.where((d >= 0) & (d <= 7), 1.0, 0.0).astype(F32)


def dot_t(a, b):
    return lax.dot_general(a, b, (((0,), (0,)), ((), ())), preferred_element_type=F32)


def gram_band(left, right, mask_ref, g_ref, out_ref):
    g_ref[0] = dot_t(left, right)
    g_ref[1] = dot_t(left, left)
    g_ref[2] = dot_t(right, right)
    for j in range(2):
        lanes = slice(128 * j, 128 * j + 128)
        acc = [jnp.zeros((8, 128), F32) for _ in range(4)]
        for t in range(-1, 17):
            u = (16 * j + t) % 32
            acc[u % 2] += g_ref[0, 8 * u : 8 * u + 8, lanes] * mask_ref[t + 1]
        for t in range(17):
            u = (16 * j + t) % 32
            mask = mask_ref[18 + t]
            acc[2 + u % 2] += g_ref[1, 8 * u : 8 * u + 8, lanes] * mask
            acc[2 + (u + 1) % 2] += g_ref[2, 8 * u : 8 * u + 8, lanes] * mask
        for r in range(4):
            out_ref[8 * r : 8 * r + 8, lanes] = acc[r]


def lane_roll(x, back):
    return pltpu.roll(x, (-back) % x.shape[1], 1)


def row_roll(x, down):
    return pltpu.roll(x, down % x.shape[0], 0)


def iota(shape, axis):
    return lax.broadcasted_iota(jnp.int32, shape, axis)


def skew(x, sign):
    c = iota(x.shape, 1)
    for b in (1, 2, 4, 8):
        x = jnp.where((c & b) != 0, row_roll(x, sign * b), x)
    return x


def spread(x):
    y = jnp.broadcast_to(x, (8, x.shape[1]))
    d = iota(y.shape, 0)
    for b in (1, 2, 4):
        y = jnp.where((d & b) != 0, lane_roll(y, b), y)
    return y


def rotation_band(band):
    cross = skew(band[:16], -1)
    own = skew(band[16:], -1)
    lr = cross[:8]
    ll = own[:8]
    rr = own[8:]
    d = iota((8, BW), 0)
    flipped = [lr[0:1]] + [lane_roll(cross[16 - k : 17 - k], k) for k in range(1, 8)]
    rl = jnp.concatenate(flipped, axis=0)
    ca = jnp.where(d == 0, 1.0, 0.0).astype(F32)
    cb = jnp.zeros((8, BW), F32)
    cc = jnp.zeros((8, BW), F32)
    cd = ca
    for r in range(ROUNDS):
        a = ll[0:1]
        c = rr[0:1]
        off = lr[0:1]
        spread_ac = c - a
        damp = (a + c) / 16.0 + 1e-06
        radius = jnp.sqrt(spread_ac * spread_ac + 4.0 * off * off + damp * damp)
        tangent = 2.0 * off / (spread_ac + radius)
        cs = 1.0 / jnp.sqrt(1.0 + tangent * tangent)
        sn = tangent * cs
        if r < ROUNDS - 1:
            csd = spread(cs)
            snd = spread(sn)
            ll1 = ll * cs - lr * sn
            lr1 = ll * sn + lr * cs
            rl1 = rl * cs - rr * sn
            rr1 = rl * sn + rr * cs
            ll = csd * ll1 - snd * rl1
            rl = snd * ll1 + csd * rl1
            lr = csd * lr1 - snd * rr1
            rr = snd * lr1 + csd * rr1
        ca, cc = cs * ca - sn * cc, sn * ca + cs * cc
        cb, cd = cs * cb - sn * cd, sn * cb + cs * cd
        if r < ROUNDS - 1:
            lr = jnp.where(d == 0, row_roll(rl, -1), row_roll(lane_roll(lr, 1), 1))
            rl = jnp.where(d == 7, 0.0, row_roll(rl, -1))
            rr = lane_roll(rr, 1)
            cc = jnp.where(d == 0, 0.0, row_roll(lane_roll(cc, 1), 1))
            cd = jnp.where(d == 0, 0.0, row_roll(lane_roll(cd, 1), 1))
    first = jnp.concatenate([ca, cb], axis=0)
    second = row_roll(jnp.concatenate([lane_roll(cd, -7), lane_roll(cc, -7)], axis=0), 1)
    return jnp.concatenate([skew(first, 1), skew(second, 1)], axis=0)


def build_dense(rot, m_ref):
    wide = rot.astype(F32)
    s = iota((16, 128), 0)
    c = iota((16, 128), 1)
    for half in range(2):
        part = wide[16 * half : 16 * half + 16]
        turned = jnp.concatenate([part[8:], part[:8]], axis=0)
        for j in range(2):
            lanes = slice(128 * j, 128 * j + 128)
            out_lanes = slice(256 * half + 128 * j, 256 * half + 128 * j + 128)
            for g in (range(0, 9) if half == 0 else range(-1, 8)):
                d = 16 * g + s - c
                keep = ((d >= 0) & (d <= 7)) if half == 0 else ((d >= -7) & (d <= 0))
                row = 16 * ((g + 8 * j) % 16)
                m_ref[row : row + 16, out_lanes] = jnp.where(keep, part[:, lanes], 0.0).astype(BF16)
                m_ref[256 + row : 256 + row + 16, out_lanes] = jnp.where(
                    keep, turned[:, lanes], 0.0
                ).astype(BF16)


def apply_dense(left, right, m_ref):
    new = jnp.dot(left, m_ref[:256], preferred_element_type=F32)
    return (new + jnp.dot(right, m_ref[256:], preferred_element_type=F32)).astype(BF16)


MESH = pl.DeviceIdType.MESH
CHUNKS = 8
TOP, LOW = slice(0, 16), slice(16, 32)


def place():
    w = lax.axis_index("wide")
    n = lax.axis_index("narrow")
    z, y_lo, core = w // 4, (w // 2) % 2, w % 2
    x, y_hi = n // 2, n % 2
    return x, 2 * y_hi + y_lo, z, core


def device(x, y, z, core):
    return ((z * 2 + y % 2) * 2 + core, x * 2 + y // 2)


def seats_before(q, pairs):
    return jnp.maximum(2 * q - 2, q), 2 * q + 3 - 3 * (q // (pairs - 1))


def block(seat):
    return pl.ds(pl.multiple_of(seat * BW, BW), BW)


def main_kernel(
    pairs,
    hold,
    x_hbm,
    y_hbm,
    rot_out,
    x_ref,
    y_ref,
    mask_ref,
    g_ref,
    m_ref,
    rot_in,
    band,
    r1,
    acc1,
    ra2,
    rb2,
    acca,
    accb,
    ra3,
    rb3,
    mine,
    rz,
    load_sem,
    store_sem,
    send_sem,
    recv_sem,
):
    half = pairs // 2
    x, y, z, core = place()
    partner = device(x, y, z, 1 - core)
    along_x = [device((x + k) % 4, y, z, core) for k in range(1, 4)]
    along_y = [device(x, (y + k) % 4, z, core) for k in range(1, 4)]
    along_z = [device(x, y, (z + k) % 8, core) for k in range(1, 8)]
    width = y_ref.shape[1] // CHUNKS

    def start(copies):
        for copy in copies:
            copy.start()

    def finish(copies):
        for copy in copies:
            copy.wait()

    loads = []
    stores = []
    for k in range(CHUNKS):
        cols = slice(k * width, (k + 1) * width)
        stores.append(pltpu.make_async_copy(y_ref.at[:, cols], y_hbm.at[:, cols], store_sem.at[k]))
    for k in range(2 * pairs):
        cols = slice(k * BW, (k + 1) * BW)
        loads.append(pltpu.make_async_copy(x_hbm.at[:, cols], x_ref.at[k], load_sem.at[k]))
    start(loads)

    barrier = pltpu.get_barrier_semaphore()
    greeted = [partner] + along_x + along_y + along_z
    for other in greeted:
        pl.semaphore_signal(barrier, inc=1, device_id=other, device_id_type=MESH)

    init_masks(mask_ref)
    m_ref[...] = jnp.zeros_like(m_ref)
    finish(loads)
    pl.semaphore_wait(barrier, len(greeted))

    for step in range(2):

        def remote(index, src, dst, target):
            return pltpu.make_async_remote_copy(
                src_ref=src,
                dst_ref=dst,
                send_sem=send_sem.at[step, index],
                recv_sem=recv_sem.at[step, index],
                device_id=target,
                device_id_type=MESH,
            )

        rot = rot_in if step == 0 else rot_out

        def gram_half(side):
            def body(i, carry):
                for k in range(2):
                    j = 2 * i + k
                    p = side * half + j
                    if step == 0:
                        left = x_ref[hold[2 * p]]
                        right = x_ref[hold[2 * p + 1]]
                    else:
                        a, b = seats_before(p, pairs)
                        left = y_ref[:, block(a)]
                        right = y_ref[:, block(b)]
                    gram_band(
                        left, right, mask_ref, g_ref.at[k], band.at[step, side, j // 4, j % 4]
                    )
                return carry

            lax.fori_loop(0, half // 2, body, 0)

        gram_half(1 - core)
        swap = [remote(0, band.at[step, 1 - core], r1.at[step], partner)]
        start(swap)
        gram_half(core)
        finish(swap)
        acc1[...] = band[step, core] + r1[step]

        copies = []
        for k in range(1, 4):
            copies.append(
                remote(k, acc1.at[(x + k) % 4, :, TOP], ra2.at[step, k - 1], along_x[k - 1])
            )
            copies.append(
                remote(3 + k, acc1.at[:, (y + k) % 4, LOW], rb2.at[step, k - 1], along_y[k - 1])
            )
        start(copies)
        finish(copies)
        acca[...] = (acc1[x, :, TOP] + ra2[step, 0]) + (ra2[step, 1] + ra2[step, 2])
        accb[...] = (acc1[:, y, LOW] + rb2[step, 0]) + (rb2[step, 1] + rb2[step, 2])

        copies = []
        for k in range(1, 4):
            copies.append(
                remote(6 + k, acca.at[(y + k) % 4], ra3.at[step, k - 1], along_y[k - 1])
            )
            copies.append(
                remote(9 + k, accb.at[(x + k) % 4], rb3.at[step, k - 1], along_x[k - 1])
            )
        start(copies)
        finish(copies)
        mine[TOP] = (acca[y] + ra3[step, 0]) + (ra3[step, 1] + ra3[step, 2])
        mine[LOW] = (accb[x] + rb3[step, 0]) + (rb3[step, 1] + rb3[step, 2])

        copies = [remote(12 + k, mine, rz.at[step, z], along_z[k - 1]) for k in range(1, 8)]
        start(copies)
        rz[step, z] = mine[...]
        finish(copies)
        total = ((rz[step, 0] + rz[step, 1]) + (rz[step, 2] + rz[step, 3])) + (
            (rz[step, 4] + rz[step, 5]) + (rz[step, 6] + rz[step, 7])
        )

        rot[core, x, y] = rotation_band(total).astype(BF16)

        copies = []
        for k in range(1, 4):
            piece = rot.at[core, x, y, TOP]
            copies.append(remote(19 + k, piece, piece, along_y[k - 1]))
            piece = rot.at[core, x, y, LOW]
            copies.append(remote(22 + k, piece, piece, along_x[k - 1]))
        start(copies)
        finish(copies)
        copies = []
        for k in range(1, 4):
            piece = rot.at[core, x, :, TOP]
            copies.append(remote(25 + k, piece, piece, along_x[k - 1]))
            piece = rot.at[core, :, y, LOW]
            copies.append(remote(28 + k, piece, piece, along_y[k - 1]))
        start(copies)
        finish(copies)
        swap = [remote(32, rot.at[core], rot.at[core], partner)]
        start(swap)
        if step == 1:
            finish(swap)
            finish(stores)
            break

        def apply_half(side):
            def body(i, carry):
                for k in range(2):
                    j = 2 * i + k
                    p = side * half + j
                    build_dense(rot[side, j // 4, j % 4], m_ref.at[k])
                    left = x_ref[hold[2 * p]]
                    right = x_ref[hold[2 * p + 1]]
                    cols = pl.ds(pl.multiple_of(p * 2 * BW, 2 * BW), 2 * BW)
                    y_ref[:, cols] = apply_dense(left, right, m_ref.at[k])
                return carry

            lax.fori_loop(0, half // 2, body, 0)

        apply_half(core)
        finish(swap)
        apply_half(1 - core)
        start(stores)


def main_call(x, holders, pairs):
    rows, cols = x.shape
    vmem = pl.BlockSpec(memory_space=pltpu.VMEM)
    hbm = pl.BlockSpec(memory_space=pl.ANY)
    out, rot = pl.pallas_call(
        functools.partial(main_kernel, pairs),
        out_shape=(
            jax.ShapeDtypeStruct((rows, cols), BF16),
            jax.ShapeDtypeStruct((2, 4, 4, 32, BW), BF16),
        ),
        in_specs=[pl.BlockSpec(memory_space=pltpu.SMEM), hbm],
        out_specs=(hbm, vmem),
        scratch_shapes=[
            pltpu.VMEM((2 * pairs, rows, BW), BF16),
            pltpu.VMEM((rows, cols), BF16),
            pltpu.VMEM((35, 8, 128), F32),
            pltpu.VMEM((2, 3, BW, BW), F32),
            pltpu.VMEM((2, 2 * BW, 2 * BW), BF16),
            pltpu.VMEM((2, 4, 4, 32, BW), BF16),
            pltpu.VMEM((2, 2, 4, 4, 32, BW), F32),
            pltpu.VMEM((2, 4, 4, 32, BW), F32),
            pltpu.VMEM((4, 4, 32, BW), F32),
            pltpu.VMEM((2, 3, 4, 16, BW), F32),
            pltpu.VMEM((2, 3, 4, 16, BW), F32),
            pltpu.VMEM((4, 16, BW), F32),
            pltpu.VMEM((4, 16, BW), F32),
            pltpu.VMEM((2, 3, 16, BW), F32),
            pltpu.VMEM((2, 3, 16, BW), F32),
            pltpu.VMEM((32, BW), F32),
            pltpu.VMEM((2, 8, 32, BW), F32),
            pltpu.SemaphoreType.DMA((2 * pairs,)),
            pltpu.SemaphoreType.DMA((CHUNKS,)),
            pltpu.SemaphoreType.DMA((2, 33)),
            pltpu.SemaphoreType.DMA((2, 33)),
        ],
        compiler_params=pltpu.CompilerParams(collective_id=0, has_side_effects=True),
    )(holders, x)
    return out, rot.reshape(pairs, 32, BW)


def last_kernel(pairs, hold, y_hbm, rot, out_hbm, y_ref, m_ref, z_ref, load_sem, store_sem):
    width = y_ref.shape[1] // CHUNKS
    per_chunk = pairs // CHUNKS

    def load(k):
        cols = pl.ds(pl.multiple_of(k * width, width), width)
        return pltpu.make_async_copy(y_hbm.at[:, cols], y_ref.at[:, cols], load_sem.at[k])

    def store(seat):
        return pltpu.make_async_copy(
            z_ref.at[:, block(seat)], out_hbm.at[:, block(hold[seat])], store_sem.at[seat]
        )

    for k in range(CHUNKS):
        load(k).start()
    m_ref[...] = jnp.zeros_like(m_ref)
    load(0).wait()

    def body(i, carry):
        @pl.when(i + 1 < CHUNKS)
        def _():
            load(i + 1).wait()

        def inner(h, carry):
            for k in range(2):
                q = i * per_chunk + 2 * h + k
                build_dense(rot[q], m_ref.at[k])
                a, b = seats_before(q, pairs)
                cols = pl.ds(pl.multiple_of(q * 2 * BW, 2 * BW), 2 * BW)
                z_ref[:, cols] = apply_dense(y_ref[:, block(a)], y_ref[:, block(b)], m_ref.at[k])
                store(2 * q).start()
                store(2 * q + 1).start()
            return carry

        return lax.fori_loop(0, per_chunk // 2, inner, carry)

    lax.fori_loop(0, CHUNKS, body, 0)

    def drain(seat, carry):
        store(seat).wait()
        return carry

    lax.fori_loop(0, 2 * pairs, drain, 0)


def last_call(y, holders, rot, pairs):
    rows, cols = y.shape
    vmem = pl.BlockSpec(memory_space=pltpu.VMEM)
    hbm = pl.BlockSpec(memory_space=pl.ANY)
    return pl.pallas_call(
        functools.partial(last_kernel, pairs),
        out_shape=jax.ShapeDtypeStruct((rows, cols), BF16),
        in_specs=[pl.BlockSpec(memory_space=pltpu.SMEM), hbm, vmem],
        out_specs=hbm,
        scratch_shapes=[
            pltpu.VMEM((rows, cols), BF16),
            pltpu.VMEM((2, 2 * BW, 2 * BW), BF16),
            pltpu.VMEM((rows, cols), BF16),
            pltpu.SemaphoreType.DMA((CHUNKS,)),
            pltpu.SemaphoreType.DMA((2 * pairs,)),
        ],
    )(holders, y, rot)


def per_device(gradient, seating):
    slots = gradient.shape[1] // BW
    pairs = slots // 2
    seat_of = seating.astype(jnp.int32)
    first = occupants(seat_of, slots)
    second = occupants(advance(seat_of, slots), slots)
    moved, rot = main_call(gradient, first, pairs)
    return last_call(moved, second, rot, pairs)


def solution(mesh):
    in_specs = (P(("wide", "narrow"), None), P())
    out_specs = P(("wide", "narrow"), None)
    return jax.shard_map(
        per_device, mesh=mesh, in_specs=in_specs, out_specs=out_specs, check_vma=False
    )
```

```python
import functools

import jax
import jax.numpy as jnp
from jax import lax
from jax.experimental import pallas as pl
from jax.experimental.pallas import tpu as pltpu
from jax.sharding import PartitionSpec as P

ROUNDS = 8
BW = 256
F32 = jnp.float32
BF16 = jnp.bfloat16


def advance(seat_of, total_slots):
    pair_count = total_slots // 2
    cycle_pos = jnp.where(seat_of % 2 == 0, seat_of // 2 - 1, total_slots - 2 - (seat_of - 1) // 2)
    next_pos = (cycle_pos + 1) % (total_slots - 1)
    new_slot = jnp.where(
        next_pos < pair_count - 1, 2 * (next_pos + 1), 2 * (total_slots - 2 - next_pos) + 1
    )
    return jnp.where(seat_of == 0, 0, new_slot)


def occupants(seat_of, total_slots):
    block_ids = jnp.arange(total_slots, dtype=jnp.int32)
    matches = seat_of[None, :] == block_ids[:, None]
    return jnp.sum(jnp.where(matches, block_ids[None, :], 0), axis=1).astype(jnp.int32)


def init_masks(mask_ref):
    s = lax.broadcasted_iota(jnp.int32, (8, 128), 0)
    c = lax.broadcasted_iota(jnp.int32, (8, 128), 1)
    for t in range(-1, 17):
        d = 8 * t + s - c
        mask_ref[t + 1] = jnp.where((d >= -7) & (d <= 7), 1.0, 0.0).astype(F32)
    for t in range(17):
        d = 8 * t + s - c
        mask_ref[18 + t] = jnp.where((d >= 0) & (d <= 7), 1.0, 0.0).astype(F32)


def dot_t(a, b):
    return lax.dot_general(a, b, (((0,), (0,)), ((), ())), preferred_element_type=F32)


def gram_band(left, right, mask_ref, g_ref, out_ref):
    g_ref[0] = dot_t(left, right)
    g_ref[1] = dot_t(left, left)
    g_ref[2] = dot_t(right, right)
    for j in range(2):
        lanes = slice(128 * j, 128 * j + 128)
        acc = [jnp.zeros((8, 128), F32) for _ in range(4)]
        for t in range(-1, 17):
            u = (16 * j + t) % 32
            acc[u % 2] += g_ref[0, 8 * u : 8 * u + 8, lanes] * mask_ref[t + 1]
        for t in range(17):
            u = (16 * j + t) % 32
            mask = mask_ref[18 + t]
            acc[2 + u % 2] += g_ref[1, 8 * u : 8 * u + 8, lanes] * mask
            acc[2 + (u + 1) % 2] += g_ref[2, 8 * u : 8 * u + 8, lanes] * mask
        for r in range(4):
            out_ref[8 * r : 8 * r + 8, lanes] = acc[r]


def lane_roll(x, back):
    return pltpu.roll(x, (-back) % x.shape[1], 1)


def row_roll(x, down):
    return pltpu.roll(x, down % x.shape[0], 0)


def iota(shape, axis):
    return lax.broadcasted_iota(jnp.int32, shape, axis)


def skew(x, sign):
    c = iota(x.shape, 1)
    for b in (1, 2, 4, 8):
        x = jnp.where((c & b) != 0, row_roll(x, sign * b), x)
    return x


def spread(x):
    y = jnp.broadcast_to(x, (8, x.shape[1]))
    d = iota(y.shape, 0)
    for b in (1, 2, 4):
        y = jnp.where((d & b) != 0, lane_roll(y, b), y)
    return y


def rotation_band(band):
    cross = skew(band[:16], -1)
    own = skew(band[16:], -1)
    lr = cross[:8]
    ll = own[:8]
    rr = own[8:]
    d = iota((8, BW), 0)
    flipped = [lr[0:1]] + [lane_roll(cross[16 - k : 17 - k], k) for k in range(1, 8)]
    rl = jnp.concatenate(flipped, axis=0)
    ca = jnp.where(d == 0, 1.0, 0.0).astype(F32)
    cb = jnp.zeros((8, BW), F32)
    cc = jnp.zeros((8, BW), F32)
    cd = ca
    for r in range(ROUNDS):
        a = ll[0:1]
        c = rr[0:1]
        off = lr[0:1]
        spread_ac = c - a
        damp = (a + c) / 16.0 + 1e-06
        radius = jnp.sqrt(spread_ac * spread_ac + 4.0 * off * off + damp * damp)
        tangent = 2.0 * off / (spread_ac + radius)
        cs = 1.0 / jnp.sqrt(1.0 + tangent * tangent)
        sn = tangent * cs
        if r < ROUNDS - 1:
            csd = spread(cs)
            snd = spread(sn)
            ll1 = ll * cs - lr * sn
            lr1 = ll * sn + lr * cs
            rl1 = rl * cs - rr * sn
            rr1 = rl * sn + rr * cs
            ll = csd * ll1 - snd * rl1
            rl = snd * ll1 + csd * rl1
            lr = csd * lr1 - snd * rr1
            rr = snd * lr1 + csd * rr1
        ca, cc = cs * ca - sn * cc, sn * ca + cs * cc
        cb, cd = cs * cb - sn * cd, sn * cb + cs * cd
        if r < ROUNDS - 1:
            lr = jnp.where(d == 0, row_roll(rl, -1), row_roll(lane_roll(lr, 1), 1))
            rl = jnp.where(d == 7, 0.0, row_roll(rl, -1))
            rr = lane_roll(rr, 1)
            cc = jnp.where(d == 0, 0.0, row_roll(lane_roll(cc, 1), 1))
            cd = jnp.where(d == 0, 0.0, row_roll(lane_roll(cd, 1), 1))
    first = jnp.concatenate([ca, cb], axis=0)
    second = row_roll(jnp.concatenate([lane_roll(cd, -7), lane_roll(cc, -7)], axis=0), 1)
    return jnp.concatenate([skew(first, 1), skew(second, 1)], axis=0)


def build_dense(rot, m_ref):
    wide = rot.astype(F32)
    s = iota((16, 128), 0)
    c = iota((16, 128), 1)
    for half in range(2):
        part = wide[16 * half : 16 * half + 16]
        turned = jnp.concatenate([part[8:], part[:8]], axis=0)
        for j in range(2):
            lanes = slice(128 * j, 128 * j + 128)
            out_lanes = slice(256 * half + 128 * j, 256 * half + 128 * j + 128)
            for g in (range(0, 9) if half == 0 else range(-1, 8)):
                d = 16 * g + s - c
                keep = ((d >= 0) & (d <= 7)) if half == 0 else ((d >= -7) & (d <= 0))
                row = 16 * ((g + 8 * j) % 16)
                m_ref[row : row + 16, out_lanes] = jnp.where(keep, part[:, lanes], 0.0).astype(BF16)
                m_ref[256 + row : 256 + row + 16, out_lanes] = jnp.where(
                    keep, turned[:, lanes], 0.0
                ).astype(BF16)


def apply_dense(left, right, m_ref):
    new = jnp.dot(left, m_ref[:256], preferred_element_type=F32)
    return (new + jnp.dot(right, m_ref[256:], preferred_element_type=F32)).astype(BF16)


MESH = pl.DeviceIdType.MESH
CHUNKS = 8
SWAP, FIRST_X, FIRST_Y, SECOND, ALONG_Z, PLANE, FORWARD, COPIES = 0, 4, 16, 32, 38, 46, 62, 78
TOP, LOW = slice(0, 16), slice(16, 32)


def place():
    w = lax.axis_index("wide")
    n = lax.axis_index("narrow")
    z, y_lo, core = w // 4, (w // 2) % 2, w % 2
    x, y_hi = n // 2, n % 2
    return x, 2 * y_hi + y_lo, z, core


def device(x, y, z, core):
    return ((z * 2 + y % 2) * 2 + core, x * 2 + y // 2)


def seats_before(q, pairs):
    return jnp.maximum(2 * q - 2, q), 2 * q + 3 - 3 * (q // (pairs - 1))


def block(seat):
    return pl.ds(pl.multiple_of(seat * BW, BW), BW)


def main_kernel(
    pairs,
    hold,
    x_hbm,
    y_hbm,
    rot_out,
    x_ref,
    y_ref,
    mask_ref,
    g_ref,
    m_ref,
    rot_in,
    band,
    r1,
    acc1,
    ra2,
    rb2,
    acca,
    accb,
    ra3,
    rb3,
    mine,
    rz,
    load_sem,
    store_sem,
    send_sem,
    recv_sem,
):
    half = pairs // 2
    x, y, z, core = place()
    partner = device(x, y, z, 1 - core)
    along_x = [device((x + k) % 4, y, z, core) for k in range(1, 4)]
    along_y = [device(x, (y + k) % 4, z, core) for k in range(1, 4)]
    along_z = [device(x, y, (z + k) % 8, core) for k in range(1, 8)]
    width = y_ref.shape[1] // CHUNKS

    def start(copies):
        for copy in copies:
            copy.start()

    def finish(copies):
        for copy in copies:
            copy.wait()

    loads = []
    stores = []
    for k in range(CHUNKS):
        cols = slice(k * width, (k + 1) * width)
        stores.append(pltpu.make_async_copy(y_ref.at[:, cols], y_hbm.at[:, cols], store_sem.at[k]))
    for k in range(2 * pairs):
        cols = slice(k * BW, (k + 1) * BW)
        loads.append(pltpu.make_async_copy(x_hbm.at[:, cols], x_ref.at[k], load_sem.at[k]))
    start(loads)

    barrier = pltpu.get_barrier_semaphore()
    plane = [device((x + i // 4) % 4, (y + i % 4) % 4, z, core) for i in range(1, 16)]
    greeted = [partner] + plane + along_z
    for other in greeted:
        pl.semaphore_signal(barrier, inc=1, device_id=other, device_id_type=MESH)

    init_masks(mask_ref)
    m_ref[...] = jnp.zeros_like(m_ref)
    finish(loads)

    for step in range(2):

        def remote(index, src, dst, target):
            return pltpu.make_async_remote_copy(
                src_ref=src,
                dst_ref=dst,
                send_sem=send_sem.at[step, index],
                recv_sem=recv_sem.at[step, index],
                device_id=target,
                device_id_type=MESH,
            )

        rot = rot_in if step == 0 else rot_out

        def gram_pairs(side, pieces):
            for k, (i, j) in enumerate(pieces):
                p = side * half + 4 * i + j
                if step == 0:
                    left = x_ref[hold[2 * p]]
                    right = x_ref[hold[2 * p + 1]]
                else:
                    a, b = seats_before(p, pairs)
                    left = y_ref[:, block(a)]
                    right = y_ref[:, block(b)]
                gram_band(left, right, mask_ref, g_ref.at[k], band.at[step, side, i, j])

        def ahead(base, i):
            return lax.rem(base + i + 1, 4)

        def swap(g):
            group = ahead(x, g)
            return remote(SWAP + g, band.at[step, 1 - core, group], r1.at[step, group], partner)

        def theirs(g, carry):
            def body(h, carry):
                gram_pairs(1 - core, [(ahead(x, g), 2 * h), (ahead(x, g), 2 * h + 1)])
                return carry

            lax.fori_loop(0, 2, body, 0)
            if step == 0:

                @pl.when(g == 0)
                def _():
                    pl.semaphore_wait(barrier, len(greeted))

            swap(g).start()
            return carry

        lax.fori_loop(0, 4, theirs, 0)

        def top(g, h):
            i, j = ahead(x, g), ahead(y, h)
            return remote(
                FIRST_X + 4 * g + h, acc1.at[i, j, TOP], ra2.at[step, g, j], device(i, y, z, core)
            )

        def low(g, h):
            i, j = ahead(x, g), ahead(y, h)
            return remote(
                FIRST_Y + 4 * g + h, acc1.at[i, j, LOW], rb2.at[step, h, i], device(x, j, z, core)
            )

        def ours(g, carry):
            i = ahead(x, g)

            def body(h2, carry):
                gram_pairs(core, [(i, ahead(y, 2 * h2)), (i, ahead(y, 2 * h2 + 1))])

                @pl.when(h2 == 0)
                def _():
                    swap(g).wait()

                for k in range(2):
                    h = 2 * h2 + k
                    j = ahead(y, h)
                    acc1[i, j] = band[step, core, i, j] + r1[step, i, j]

                    @pl.when(g < 3)
                    def _():
                        top(g, h).start()

                    @pl.when(h < 3)
                    def _():
                        low(g, h).start()

                return carry

            return lax.fori_loop(0, 2, body, carry)

        lax.fori_loop(0, 4, ours, 0)

        def arrived(n, carry):
            a, b = n // 4, lax.rem(n, 4)
            top(a, b).wait()
            low(b, a).wait()
            return carry

        lax.fori_loop(0, 12, arrived, 0)
        acca[...] = (acc1[x, :, TOP] + ra2[step, 0]) + (ra2[step, 1] + ra2[step, 2])
        accb[...] = (acc1[:, y, LOW] + rb2[step, 0]) + (rb2[step, 1] + rb2[step, 2])

        copies = []
        for k in range(1, 4):
            copies.append(
                remote(SECOND + k, acca.at[(y + k) % 4], ra3.at[step, k - 1], along_y[k - 1])
            )
            copies.append(
                remote(SECOND + 3 + k, accb.at[(x + k) % 4], rb3.at[step, k - 1], along_x[k - 1])
            )
        start(copies)
        finish(copies)
        mine[TOP] = (acca[y] + ra3[step, 0]) + (ra3[step, 1] + ra3[step, 2])
        mine[LOW] = (accb[x] + rb3[step, 0]) + (rb3[step, 1] + rb3[step, 2])

        copies = [remote(ALONG_Z + k, mine, rz.at[step, z], along_z[k - 1]) for k in range(1, 8)]
        start(copies)
        rz[step, z] = mine[...]
        finish(copies)
        total = ((rz[step, 0] + rz[step, 1]) + (rz[step, 2] + rz[step, 3])) + (
            (rz[step, 4] + rz[step, 5]) + (rz[step, 6] + rz[step, 7])
        )

        rot[core, x, y] = rotation_band(total).astype(BF16)

        def spread_out(i):
            piece = rot.at[core, x, y]
            return remote(PLANE + i, piece, piece, device((x + i // 4) % 4, (y + i % 4) % 4, z, core))

        def source(i):
            return lax.rem(x + 4 - i // 4, 4), lax.rem(y + 4 - lax.rem(i, 4), 4)

        def arriving(i):
            sx, sy = source(i)
            piece = rot.at[core, sx, sy]
            return remote(PLANE + i, piece, piece, partner)

        def forward(i):
            sx, sy = source(i)
            piece = rot.at[core, sx, sy]
            return remote(FORWARD + i, piece, piece, partner)

        def forwarded(i):
            sx, sy = source(i)
            piece = rot.at[1 - core, sx, sy]
            return remote(FORWARD + i, piece, piece, partner)

        for i in range(1, 16):
            spread_out(i).start()
        forward(0).start()

        def apply_pair(side, i, k):
            sx, sy = source(i)
            p = side * half + 4 * sx + sy
            build_dense(rot[side, sx, sy], m_ref.at[k])
            left = x_ref[hold[2 * p]]
            right = x_ref[hold[2 * p + 1]]
            cols = pl.ds(pl.multiple_of(p * 2 * BW, 2 * BW), 2 * BW)
            y_ref[:, cols] = apply_dense(left, right, m_ref.at[k])

        def first_half(h, carry):
            for k in range(2):
                i = 2 * h + k

                @pl.when(i > 0)
                def _():
                    arriving(i).wait_recv()
                    forward(i).start()

            if step == 0:
                for k in range(2):
                    apply_pair(core, 2 * h + k, k)
            return carry

        def second_half(h, carry):
            for k in range(2):
                forwarded(2 * h + k).wait_recv()
            if step == 0:
                for k in range(2):
                    apply_pair(1 - core, 2 * h + k, k)
            return carry

        lax.fori_loop(0, 8, first_half, 0)
        lax.fori_loop(0, 8, second_half, 0)
        for i in range(1, 16):
            spread_out(i).wait_send()
        for i in range(16):
            forward(i).wait_send()
        if step == 0:
            start(stores)
    finish(stores)


def main_call(x, holders, pairs):
    rows, cols = x.shape
    vmem = pl.BlockSpec(memory_space=pltpu.VMEM)
    hbm = pl.BlockSpec(memory_space=pl.ANY)
    out, rot = pl.pallas_call(
        functools.partial(main_kernel, pairs),
        out_shape=(
            jax.ShapeDtypeStruct((rows, cols), BF16),
            jax.ShapeDtypeStruct((2, 4, 4, 32, BW), BF16),
        ),
        in_specs=[pl.BlockSpec(memory_space=pltpu.SMEM), hbm],
        out_specs=(hbm, vmem),
        scratch_shapes=[
            pltpu.VMEM((2 * pairs, rows, BW), BF16),
            pltpu.VMEM((rows, cols), BF16),
            pltpu.VMEM((35, 8, 128), F32),
            pltpu.VMEM((2, 3, BW, BW), F32),
            pltpu.VMEM((2, 2 * BW, 2 * BW), BF16),
            pltpu.VMEM((2, 4, 4, 32, BW), BF16),
            pltpu.VMEM((2, 2, 4, 4, 32, BW), F32),
            pltpu.VMEM((2, 4, 4, 32, BW), F32),
            pltpu.VMEM((4, 4, 32, BW), F32),
            pltpu.VMEM((2, 3, 4, 16, BW), F32),
            pltpu.VMEM((2, 3, 4, 16, BW), F32),
            pltpu.VMEM((4, 16, BW), F32),
            pltpu.VMEM((4, 16, BW), F32),
            pltpu.VMEM((2, 3, 16, BW), F32),
            pltpu.VMEM((2, 3, 16, BW), F32),
            pltpu.VMEM((32, BW), F32),
            pltpu.VMEM((2, 8, 32, BW), F32),
            pltpu.SemaphoreType.DMA((2 * pairs,)),
            pltpu.SemaphoreType.DMA((CHUNKS,)),
            pltpu.SemaphoreType.DMA((2, COPIES)),
            pltpu.SemaphoreType.DMA((2, COPIES)),
        ],
        compiler_params=pltpu.CompilerParams(collective_id=0, has_side_effects=True),
    )(holders, x)
    return out, rot.reshape(pairs, 32, BW)


def last_kernel(pairs, hold, y_hbm, rot, out_hbm, y_ref, m_ref, z_ref, load_sem, store_sem):
    width = y_ref.shape[1] // CHUNKS
    per_chunk = pairs // CHUNKS

    def load(k):
        cols = pl.ds(pl.multiple_of(k * width, width), width)
        return pltpu.make_async_copy(y_hbm.at[:, cols], y_ref.at[:, cols], load_sem.at[k])

    def store(seat):
        return pltpu.make_async_copy(
            z_ref.at[:, block(seat)], out_hbm.at[:, block(hold[seat])], store_sem.at[seat]
        )

    for k in range(CHUNKS):
        load(k).start()
    m_ref[...] = jnp.zeros_like(m_ref)
    load(0).wait()

    def body(i, carry):
        @pl.when(i + 1 < CHUNKS)
        def _():
            load(i + 1).wait()

        def inner(h, carry):
            for k in range(2):
                q = i * per_chunk + 2 * h + k
                build_dense(rot[q], m_ref.at[k])
                a, b = seats_before(q, pairs)
                cols = pl.ds(pl.multiple_of(q * 2 * BW, 2 * BW), 2 * BW)
                z_ref[:, cols] = apply_dense(y_ref[:, block(a)], y_ref[:, block(b)], m_ref.at[k])
                store(2 * q).start()
                store(2 * q + 1).start()
            return carry

        return lax.fori_loop(0, per_chunk // 2, inner, carry)

    lax.fori_loop(0, CHUNKS, body, 0)

    def drain(seat, carry):
        store(seat).wait()
        return carry

    lax.fori_loop(0, 2 * pairs, drain, 0)


def last_call(y, holders, rot, pairs):
    rows, cols = y.shape
    vmem = pl.BlockSpec(memory_space=pltpu.VMEM)
    hbm = pl.BlockSpec(memory_space=pl.ANY)
    return pl.pallas_call(
        functools.partial(last_kernel, pairs),
        out_shape=jax.ShapeDtypeStruct((rows, cols), BF16),
        in_specs=[pl.BlockSpec(memory_space=pltpu.SMEM), hbm, vmem],
        out_specs=hbm,
        scratch_shapes=[
            pltpu.VMEM((rows, cols), BF16),
            pltpu.VMEM((2, 2 * BW, 2 * BW), BF16),
            pltpu.VMEM((rows, cols), BF16),
            pltpu.SemaphoreType.DMA((CHUNKS,)),
            pltpu.SemaphoreType.DMA((2 * pairs,)),
        ],
    )(holders, y, rot)


def per_device(gradient, seating):
    slots = gradient.shape[1] // BW
    pairs = slots // 2
    seat_of = seating.astype(jnp.int32)
    first = occupants(seat_of, slots)
    second = occupants(advance(seat_of, slots), slots)
    moved, rot = main_call(gradient, first, pairs)
    return last_call(moved, second, rot, pairs)


def solution(mesh):
    in_specs = (P(("wide", "narrow"), None), P())
    out_specs = P(("wide", "narrow"), None)
    return jax.shard_map(
        per_device, mesh=mesh, in_specs=in_specs, out_specs=out_specs, check_vma=False
    )
```

```python
import functools

import jax
import jax.numpy as jnp
from jax import lax
from jax.experimental import pallas as pl
from jax.experimental.pallas import tpu as pltpu
from jax.sharding import PartitionSpec as P

ROUNDS = 8
BW = 256
F32 = jnp.float32
BF16 = jnp.bfloat16


def advance(seat_of, total_slots):
    pair_count = total_slots // 2
    cycle_pos = jnp.where(seat_of % 2 == 0, seat_of // 2 - 1, total_slots - 2 - (seat_of - 1) // 2)
    next_pos = (cycle_pos + 1) % (total_slots - 1)
    new_slot = jnp.where(
        next_pos < pair_count - 1, 2 * (next_pos + 1), 2 * (total_slots - 2 - next_pos) + 1
    )
    return jnp.where(seat_of == 0, 0, new_slot)


def occupants(seat_of, total_slots):
    block_ids = jnp.arange(total_slots, dtype=jnp.int32)
    matches = seat_of[None, :] == block_ids[:, None]
    return jnp.sum(jnp.where(matches, block_ids[None, :], 0), axis=1).astype(jnp.int32)


def init_masks(mask_ref):
    s = lax.broadcasted_iota(jnp.int32, (8, 128), 0)
    c = lax.broadcasted_iota(jnp.int32, (8, 128), 1)
    for t in range(-1, 17):
        d = 8 * t + s - c
        mask_ref[t + 1] = jnp.where((d >= -7) & (d <= 7), 1.0, 0.0).astype(F32)
    for t in range(17):
        d = 8 * t + s - c
        mask_ref[18 + t] = jnp.where((d >= 0) & (d <= 7), 1.0, 0.0).astype(F32)


def dot_t(a, b):
    return lax.dot_general(a, b, (((0,), (0,)), ((), ())), preferred_element_type=F32)


def gram_band(left, right, mask_ref, g_ref, out_ref):
    g_ref[0] = dot_t(left, right)
    g_ref[1] = dot_t(left, left)
    g_ref[2] = dot_t(right, right)
    for j in range(2):
        lanes = slice(128 * j, 128 * j + 128)
        acc = [jnp.zeros((8, 128), F32) for _ in range(4)]
        for t in range(-1, 17):
            u = (16 * j + t) % 32
            acc[u % 2] += g_ref[0, 8 * u : 8 * u + 8, lanes] * mask_ref[t + 1]
        for t in range(17):
            u = (16 * j + t) % 32
            mask = mask_ref[18 + t]
            acc[2 + u % 2] += g_ref[1, 8 * u : 8 * u + 8, lanes] * mask
            acc[2 + (u + 1) % 2] += g_ref[2, 8 * u : 8 * u + 8, lanes] * mask
        for r in range(4):
            out_ref[8 * r : 8 * r + 8, lanes] = acc[r]


def lane_roll(x, back):
    return pltpu.roll(x, (-back) % x.shape[1], 1)


def row_roll(x, down):
    return pltpu.roll(x, down % x.shape[0], 0)


def iota(shape, axis):
    return lax.broadcasted_iota(jnp.int32, shape, axis)


def skew(x, sign):
    c = iota(x.shape, 1)
    for b in (1, 2, 4, 8):
        x = jnp.where((c & b) != 0, row_roll(x, sign * b), x)
    return x


def spread(x):
    y = jnp.broadcast_to(x, (8, x.shape[1]))
    d = iota(y.shape, 0)
    for b in (1, 2, 4):
        y = jnp.where((d & b) != 0, lane_roll(y, b), y)
    return y


def rotation_band(band):
    cross = skew(band[:16], -1)
    own = skew(band[16:], -1)
    lr = cross[:8]
    ll = own[:8]
    rr = own[8:]
    d = iota((8, BW), 0)
    flipped = [lr[0:1]] + [lane_roll(cross[16 - k : 17 - k], k) for k in range(1, 8)]
    rl = jnp.concatenate(flipped, axis=0)
    ca = jnp.where(d == 0, 1.0, 0.0).astype(F32)
    cb = jnp.zeros((8, BW), F32)
    cc = jnp.zeros((8, BW), F32)
    cd = ca
    for r in range(ROUNDS):
        a = ll[0:1]
        c = rr[0:1]
        off = lr[0:1]
        spread_ac = c - a
        damp = (a + c) / 16.0 + 1e-06
        radius = jnp.sqrt(spread_ac * spread_ac + 4.0 * off * off + damp * damp)
        tangent = 2.0 * off / (spread_ac + radius)
        cs = 1.0 / jnp.sqrt(1.0 + tangent * tangent)
        sn = tangent * cs
        if r < ROUNDS - 1:
            csd = spread(cs)
            snd = spread(sn)
            ll1 = ll * cs - lr * sn
            lr1 = ll * sn + lr * cs
            rl1 = rl * cs - rr * sn
            rr1 = rl * sn + rr * cs
            ll = csd * ll1 - snd * rl1
            rl = snd * ll1 + csd * rl1
            lr = csd * lr1 - snd * rr1
            rr = snd * lr1 + csd * rr1
        ca, cc = cs * ca - sn * cc, sn * ca + cs * cc
        cb, cd = cs * cb - sn * cd, sn * cb + cs * cd
        if r < ROUNDS - 1:
            lr = jnp.where(d == 0, row_roll(rl, -1), row_roll(lane_roll(lr, 1), 1))
            rl = jnp.where(d == 7, 0.0, row_roll(rl, -1))
            rr = lane_roll(rr, 1)
            cc = jnp.where(d == 0, 0.0, row_roll(lane_roll(cc, 1), 1))
            cd = jnp.where(d == 0, 0.0, row_roll(lane_roll(cd, 1), 1))
    first = jnp.concatenate([ca, cb], axis=0)
    second = row_roll(jnp.concatenate([lane_roll(cd, -7), lane_roll(cc, -7)], axis=0), 1)
    return jnp.concatenate([skew(first, 1), skew(second, 1)], axis=0)


def init_keep(keep_ref):
    s = lax.broadcasted_iota(jnp.int32, (16, 128), 0)
    c = lax.broadcasted_iota(jnp.int32, (16, 128), 1)
    for t in range(9):
        d = 16 * t + s - c
        keep_ref[t] = jnp.where((d >= 0) & (d <= 7), 1.0, 0.0).astype(BF16)
        d = 16 * (t - 1) + s - c
        keep_ref[9 + t] = jnp.where((d >= -7) & (d <= 0), 1.0, 0.0).astype(BF16)


def build_dense(rot, keep_ref, m_ref):
    for half in range(2):
        part = rot[16 * half : 16 * half + 16]
        turned = part.astype(F32)
        turned = jnp.concatenate([turned[8:], turned[:8]], axis=0).astype(BF16)
        for j in range(2):
            lanes = slice(128 * j, 128 * j + 128)
            out_lanes = slice(256 * half + 128 * j, 256 * half + 128 * j + 128)
            for t in range(9):
                row = 16 * ((t - half + 8 * j) % 16)
                keep = keep_ref[9 * half + t]
                m_ref[row : row + 16, out_lanes] = part[:, lanes] * keep
                m_ref[256 + row : 256 + row + 16, out_lanes] = turned[:, lanes] * keep


def apply_dense(left, right, m_ref):
    new = jnp.dot(left, m_ref[:256], preferred_element_type=F32)
    return (new + jnp.dot(right, m_ref[256:], preferred_element_type=F32)).astype(BF16)


MESH = pl.DeviceIdType.MESH
CHUNKS = 8
SWAP, FIRST_X, FIRST_Y, SECOND, ALONG_Z, PLANE, FORWARD, COPIES = 0, 4, 16, 32, 38, 46, 62, 78
TOP, LOW = slice(0, 16), slice(16, 32)


def place():
    w = lax.axis_index("wide")
    n = lax.axis_index("narrow")
    z, y_lo, core = w // 4, (w // 2) % 2, w % 2
    x, y_hi = n // 2, n % 2
    return x, 2 * y_hi + y_lo, z, core


def device(x, y, z, core):
    return ((z * 2 + y % 2) * 2 + core, x * 2 + y // 2)


def seats_before(q, pairs):
    return jnp.maximum(2 * q - 2, q), 2 * q + 3 - 3 * (q // (pairs - 1))


def block(seat):
    return pl.ds(pl.multiple_of(seat * BW, BW), BW)


def main_kernel(
    pairs,
    hold,
    x_hbm,
    y_hbm,
    rot_out,
    x_ref,
    y_ref,
    mask_ref,
    g_ref,
    keep_ref,
    m_ref,
    rot_in,
    band,
    r1,
    acc1,
    ra2,
    rb2,
    acca,
    accb,
    ra3,
    rb3,
    mine,
    rz,
    load_sem,
    store_sem,
    send_sem,
    recv_sem,
):
    half = pairs // 2
    x, y, z, core = place()
    partner = device(x, y, z, 1 - core)
    along_x = [device((x + k) % 4, y, z, core) for k in range(1, 4)]
    along_y = [device(x, (y + k) % 4, z, core) for k in range(1, 4)]
    along_z = [device(x, y, (z + k) % 8, core) for k in range(1, 8)]
    width = y_ref.shape[1] // CHUNKS

    def start(copies):
        for copy in copies:
            copy.start()

    def finish(copies):
        for copy in copies:
            copy.wait()

    loads = []
    stores = []
    for k in range(CHUNKS):
        cols = slice(k * width, (k + 1) * width)
        stores.append(pltpu.make_async_copy(y_ref.at[:, cols], y_hbm.at[:, cols], store_sem.at[k]))
    for k in range(2 * pairs):
        cols = slice(k * BW, (k + 1) * BW)
        loads.append(pltpu.make_async_copy(x_hbm.at[:, cols], x_ref.at[k], load_sem.at[k]))
    start(loads)

    barrier = pltpu.get_barrier_semaphore()
    plane = [device((x + i // 4) % 4, (y + i % 4) % 4, z, core) for i in range(1, 16)]
    greeted = [partner] + plane + along_z
    for other in greeted:
        pl.semaphore_signal(barrier, inc=1, device_id=other, device_id_type=MESH)

    init_masks(mask_ref)
    init_keep(keep_ref)
    m_ref[...] = jnp.zeros_like(m_ref)
    finish(loads)

    for step in range(2):

        def remote(index, src, dst, target):
            return pltpu.make_async_remote_copy(
                src_ref=src,
                dst_ref=dst,
                send_sem=send_sem.at[step, index],
                recv_sem=recv_sem.at[step, index],
                device_id=target,
                device_id_type=MESH,
            )

        rot = rot_in if step == 0 else rot_out

        def gram_pairs(side, pieces):
            for k, (i, j) in enumerate(pieces):
                p = side * half + 4 * i + j
                if step == 0:
                    left = x_ref[hold[2 * p]]
                    right = x_ref[hold[2 * p + 1]]
                else:
                    a, b = seats_before(p, pairs)
                    left = y_ref[:, block(a)]
                    right = y_ref[:, block(b)]
                gram_band(left, right, mask_ref, g_ref.at[k], band.at[step, side, i, j])

        def ahead(base, i):
            return lax.rem(base + i + 1, 4)

        def swap(g):
            group = ahead(x, g)
            return remote(SWAP + g, band.at[step, 1 - core, group], r1.at[step, group], partner)

        def theirs(g, carry):
            gram_pairs(1 - core, [(ahead(x, g), j) for j in range(4)])
            if step == 0:

                @pl.when(g == 0)
                def _():
                    pl.semaphore_wait(barrier, len(greeted))

            swap(g).start()
            return carry

        lax.fori_loop(0, 4, theirs, 0)

        def top(g, h):
            i, j = ahead(x, g), ahead(y, h)
            return remote(
                FIRST_X + 4 * g + h, acc1.at[i, j, TOP], ra2.at[step, g, j], device(i, y, z, core)
            )

        def low(g, h):
            i, j = ahead(x, g), ahead(y, h)
            return remote(
                FIRST_Y + 4 * g + h, acc1.at[i, j, LOW], rb2.at[step, h, i], device(x, j, z, core)
            )

        def ours(g, carry):
            i = ahead(x, g)

            gram_pairs(core, [(i, ahead(y, h)) for h in range(4)])
            swap(g).wait()
            for h in range(4):
                j = ahead(y, h)
                acc1[i, j] = band[step, core, i, j] + r1[step, i, j]

                @pl.when(g < 3)
                def _():
                    top(g, h).start()

                if h < 3:
                    low(g, h).start()
            return carry

        lax.fori_loop(0, 4, ours, 0)

        def arrived(n, carry):
            a, b = n // 4, lax.rem(n, 4)
            top(a, b).wait()
            low(b, a).wait()
            return carry

        lax.fori_loop(0, 12, arrived, 0)
        acca[...] = (acc1[x, :, TOP] + ra2[step, 0]) + (ra2[step, 1] + ra2[step, 2])
        accb[...] = (acc1[:, y, LOW] + rb2[step, 0]) + (rb2[step, 1] + rb2[step, 2])

        copies = []
        for k in range(1, 4):
            copies.append(
                remote(SECOND + k, acca.at[(y + k) % 4], ra3.at[step, k - 1], along_y[k - 1])
            )
            copies.append(
                remote(SECOND + 3 + k, accb.at[(x + k) % 4], rb3.at[step, k - 1], along_x[k - 1])
            )
        start(copies)
        finish(copies)
        mine[TOP] = (acca[y] + ra3[step, 0]) + (ra3[step, 1] + ra3[step, 2])
        mine[LOW] = (accb[x] + rb3[step, 0]) + (rb3[step, 1] + rb3[step, 2])

        copies = [remote(ALONG_Z + k, mine, rz.at[step, z], along_z[k - 1]) for k in range(1, 8)]
        start(copies)
        rz[step, z] = mine[...]
        finish(copies)
        total = ((rz[step, 0] + rz[step, 1]) + (rz[step, 2] + rz[step, 3])) + (
            (rz[step, 4] + rz[step, 5]) + (rz[step, 6] + rz[step, 7])
        )

        rot[core, x, y] = rotation_band(total).astype(BF16)

        def spread_out(i):
            piece = rot.at[core, x, y]
            return remote(PLANE + i, piece, piece, device((x + i // 4) % 4, (y + i % 4) % 4, z, core))

        def source(i):
            return lax.rem(x + 4 - i // 4, 4), lax.rem(y + 4 - lax.rem(i, 4), 4)

        def arriving(i):
            sx, sy = source(i)
            piece = rot.at[core, sx, sy]
            return remote(PLANE + i, piece, piece, partner)

        def forward(i):
            sx, sy = source(i)
            piece = rot.at[core, sx, sy]
            return remote(FORWARD + i, piece, piece, partner)

        def forwarded(i):
            sx, sy = source(i)
            piece = rot.at[1 - core, sx, sy]
            return remote(FORWARD + i, piece, piece, partner)

        for i in range(1, 16):
            spread_out(i).start()
        forward(0).start()

        def apply_pair(side, i, k):
            sx, sy = source(i)
            p = side * half + 4 * sx + sy
            build_dense(rot[side, sx, sy], keep_ref, m_ref.at[k])
            left = x_ref[hold[2 * p]]
            right = x_ref[hold[2 * p + 1]]
            cols = pl.ds(pl.multiple_of(p * 2 * BW, 2 * BW), 2 * BW)
            y_ref[:, cols] = apply_dense(left, right, m_ref.at[k])

        def first_half(h, carry):
            for k in range(4):
                i = 4 * h + k

                @pl.when(i > 0)
                def _():
                    arriving(i).wait_recv()
                    forward(i).start()

            if step == 0:
                for k in range(4):
                    apply_pair(core, 4 * h + k, k)
            return carry

        def second_half(h, carry):
            for k in range(4):
                forwarded(4 * h + k).wait_recv()
            if step == 0:
                for k in range(4):
                    apply_pair(1 - core, 4 * h + k, k)
            return carry

        lax.fori_loop(0, 4, first_half, 0)
        lax.fori_loop(0, 4, second_half, 0)
        for i in range(1, 16):
            spread_out(i).wait_send()
        for i in range(16):
            forward(i).wait_send()
        if step == 0:
            start(stores)
    finish(stores)


def main_call(x, holders, pairs):
    rows, cols = x.shape
    vmem = pl.BlockSpec(memory_space=pltpu.VMEM)
    hbm = pl.BlockSpec(memory_space=pl.ANY)
    out, rot = pl.pallas_call(
        functools.partial(main_kernel, pairs),
        out_shape=(
            jax.ShapeDtypeStruct((rows, cols), BF16),
            jax.ShapeDtypeStruct((2, 4, 4, 32, BW), BF16),
        ),
        in_specs=[pl.BlockSpec(memory_space=pltpu.SMEM), hbm],
        out_specs=(hbm, vmem),
        scratch_shapes=[
            pltpu.VMEM((2 * pairs, rows, BW), BF16),
            pltpu.VMEM((rows, cols), BF16),
            pltpu.VMEM((35, 8, 128), F32),
            pltpu.VMEM((4, 3, BW, BW), F32),
            pltpu.VMEM((18, 16, 128), BF16),
            pltpu.VMEM((4, 2 * BW, 2 * BW), BF16),
            pltpu.VMEM((2, 4, 4, 32, BW), BF16),
            pltpu.VMEM((2, 2, 4, 4, 32, BW), F32),
            pltpu.VMEM((2, 4, 4, 32, BW), F32),
            pltpu.VMEM((4, 4, 32, BW), F32),
            pltpu.VMEM((2, 3, 4, 16, BW), F32),
            pltpu.VMEM((2, 3, 4, 16, BW), F32),
            pltpu.VMEM((4, 16, BW), F32),
            pltpu.VMEM((4, 16, BW), F32),
            pltpu.VMEM((2, 3, 16, BW), F32),
            pltpu.VMEM((2, 3, 16, BW), F32),
            pltpu.VMEM((32, BW), F32),
            pltpu.VMEM((2, 8, 32, BW), F32),
            pltpu.SemaphoreType.DMA((2 * pairs,)),
            pltpu.SemaphoreType.DMA((CHUNKS,)),
            pltpu.SemaphoreType.DMA((2, COPIES)),
            pltpu.SemaphoreType.DMA((2, COPIES)),
        ],
        compiler_params=pltpu.CompilerParams(collective_id=0, has_side_effects=True),
    )(holders, x)
    return out, rot.reshape(pairs, 32, BW)


def last_kernel(
    pairs, hold, y_hbm, rot, out_hbm, y_ref, keep_ref, m_ref, z_ref, load_sem, store_sem
):
    width = y_ref.shape[1] // CHUNKS
    per_chunk = pairs // CHUNKS

    def load(k):
        cols = pl.ds(pl.multiple_of(k * width, width), width)
        return pltpu.make_async_copy(y_hbm.at[:, cols], y_ref.at[:, cols], load_sem.at[k])

    def store(seat):
        return pltpu.make_async_copy(
            z_ref.at[:, block(seat)], out_hbm.at[:, block(hold[seat])], store_sem.at[seat]
        )

    for k in range(CHUNKS):
        load(k).start()
    init_keep(keep_ref)
    m_ref[...] = jnp.zeros_like(m_ref)
    load(0).wait()

    def body(i, carry):
        @pl.when(i + 1 < CHUNKS)
        def _():
            load(i + 1).wait()

        def inner(h, carry):
            for k in range(4):
                q = i * per_chunk + 4 * h + k
                build_dense(rot[q], keep_ref, m_ref.at[k])
                a, b = seats_before(q, pairs)
                cols = pl.ds(pl.multiple_of(q * 2 * BW, 2 * BW), 2 * BW)
                z_ref[:, cols] = apply_dense(y_ref[:, block(a)], y_ref[:, block(b)], m_ref.at[k])
                store(2 * q).start()
                store(2 * q + 1).start()
            return carry

        return lax.fori_loop(0, per_chunk // 4, inner, carry)

    lax.fori_loop(0, CHUNKS, body, 0)

    def drain(seat, carry):
        store(seat).wait()
        return carry

    lax.fori_loop(0, 2 * pairs, drain, 0)


def last_call(y, holders, rot, pairs):
    rows, cols = y.shape
    vmem = pl.BlockSpec(memory_space=pltpu.VMEM)
    hbm = pl.BlockSpec(memory_space=pl.ANY)
    return pl.pallas_call(
        functools.partial(last_kernel, pairs),
        out_shape=jax.ShapeDtypeStruct((rows, cols), BF16),
        in_specs=[pl.BlockSpec(memory_space=pltpu.SMEM), hbm, vmem],
        out_specs=hbm,
        scratch_shapes=[
            pltpu.VMEM((rows, cols), BF16),
            pltpu.VMEM((18, 16, 128), BF16),
            pltpu.VMEM((4, 2 * BW, 2 * BW), BF16),
            pltpu.VMEM((rows, cols), BF16),
            pltpu.SemaphoreType.DMA((CHUNKS,)),
            pltpu.SemaphoreType.DMA((2 * pairs,)),
        ],
    )(holders, y, rot)


def per_device(gradient, seating):
    slots = gradient.shape[1] // BW
    pairs = slots // 2
    seat_of = seating.astype(jnp.int32)
    first = occupants(seat_of, slots)
    second = occupants(advance(seat_of, slots), slots)
    moved, rot = main_call(gradient, first, pairs)
    return last_call(moved, second, rot, pairs)


def solution(mesh):
    in_specs = (P(("wide", "narrow"), None), P())
    out_specs = P(("wide", "narrow"), None)
    return jax.shard_map(
        per_device, mesh=mesh, in_specs=in_specs, out_specs=out_specs, check_vma=False
    )
```

```python
import functools

import jax
import jax.numpy as jnp
from jax import lax
from jax.experimental import pallas as pl
from jax.experimental.pallas import tpu as pltpu
from jax.sharding import PartitionSpec as P

ROUNDS = 8
BW = 256
F32 = jnp.float32
BF16 = jnp.bfloat16


def occupants(seat_of, total_slots):
    block_ids = jnp.arange(total_slots, dtype=jnp.int32)
    matches = seat_of[None, :] == block_ids[:, None]
    return jnp.sum(jnp.where(matches, block_ids[None, :], 0), axis=1).astype(jnp.int32)


def init_masks(mask_ref):
    s = lax.broadcasted_iota(jnp.int32, (8, 128), 0)
    c = lax.broadcasted_iota(jnp.int32, (8, 128), 1)
    for t in range(-1, 17):
        d = 8 * t + s - c
        mask_ref[t + 1] = jnp.where((d >= -7) & (d <= 7), 1.0, 0.0).astype(F32)
    for t in range(17):
        d = 8 * t + s - c
        mask_ref[18 + t] = jnp.where((d >= 0) & (d <= 7), 1.0, 0.0).astype(F32)


def dot_t(a, b):
    return lax.dot_general(a, b, (((0,), (0,)), ((), ())), preferred_element_type=F32)


def gram_band(left, right, mask_ref, g_ref, out_ref):
    g_ref[0] = dot_t(left, right)
    g_ref[1] = dot_t(left, left)
    g_ref[2] = dot_t(right, right)
    for j in range(2):
        lanes = slice(128 * j, 128 * j + 128)
        acc = [jnp.zeros((8, 128), F32) for _ in range(4)]
        for t in range(-1, 17):
            u = (16 * j + t) % 32
            acc[u % 2] += g_ref[0, 8 * u : 8 * u + 8, lanes] * mask_ref[t + 1]
        for t in range(17):
            u = (16 * j + t) % 32
            mask = mask_ref[18 + t]
            acc[2 + u % 2] += g_ref[1, 8 * u : 8 * u + 8, lanes] * mask
            acc[2 + (u + 1) % 2] += g_ref[2, 8 * u : 8 * u + 8, lanes] * mask
        for r in range(4):
            out_ref[8 * r : 8 * r + 8, lanes] = acc[r]


def lane_roll(x, back):
    return pltpu.roll(x, (-back) % x.shape[1], 1)


def row_roll(x, down):
    return pltpu.roll(x, down % x.shape[0], 0)


def iota(shape, axis):
    return lax.broadcasted_iota(jnp.int32, shape, axis)


def skew(x, sign):
    c = iota(x.shape, 1)
    for b in (1, 2, 4, 8):
        x = jnp.where((c & b) != 0, row_roll(x, sign * b), x)
    return x


def spread(x):
    y = jnp.broadcast_to(x, (8, x.shape[1]))
    d = iota(y.shape, 0)
    for b in (1, 2, 4):
        y = jnp.where((d & b) != 0, lane_roll(y, b), y)
    return y


def rotation_band(band):
    cross = skew(band[:16], -1)
    own = skew(band[16:], -1)
    lr = cross[:8]
    ll = own[:8]
    rr = own[8:]
    d = iota((8, BW), 0)
    flipped = [lr[0:1]] + [lane_roll(cross[16 - k : 17 - k], k) for k in range(1, 8)]
    rl = jnp.concatenate(flipped, axis=0)
    ca = jnp.where(d == 0, 1.0, 0.0).astype(F32)
    cb = jnp.zeros((8, BW), F32)
    cc = jnp.zeros((8, BW), F32)
    cd = ca
    for r in range(ROUNDS):
        a = ll[0:1]
        c = rr[0:1]
        off = lr[0:1]
        spread_ac = c - a
        damp = (a + c) / 16.0 + 1e-06
        radius = jnp.sqrt(spread_ac * spread_ac + 4.0 * off * off + damp * damp)
        tangent = 2.0 * off / (spread_ac + radius)
        cs = 1.0 / jnp.sqrt(1.0 + tangent * tangent)
        sn = tangent * cs
        if r < ROUNDS - 1:
            csd = spread(cs)
            snd = spread(sn)
            ll1 = ll * cs - lr * sn
            lr1 = ll * sn + lr * cs
            rl1 = rl * cs - rr * sn
            rr1 = rl * sn + rr * cs
            ll = csd * ll1 - snd * rl1
            rl = snd * ll1 + csd * rl1
            lr = csd * lr1 - snd * rr1
            rr = snd * lr1 + csd * rr1
        ca, cc = cs * ca - sn * cc, sn * ca + cs * cc
        cb, cd = cs * cb - sn * cd, sn * cb + cs * cd
        if r < ROUNDS - 1:
            lr = jnp.where(d == 0, row_roll(rl, -1), row_roll(lane_roll(lr, 1), 1))
            rl = jnp.where(d == 7, 0.0, row_roll(rl, -1))
            rr = lane_roll(rr, 1)
            cc = jnp.where(d == 0, 0.0, row_roll(lane_roll(cc, 1), 1))
            cd = jnp.where(d == 0, 0.0, row_roll(lane_roll(cd, 1), 1))
    first = jnp.concatenate([ca, cb], axis=0)
    second = row_roll(jnp.concatenate([lane_roll(cd, -7), lane_roll(cc, -7)], axis=0), 1)
    return jnp.concatenate([skew(first, 1), skew(second, 1)], axis=0)


def init_keep(keep_ref):
    s = lax.broadcasted_iota(jnp.int32, (16, 128), 0)
    c = lax.broadcasted_iota(jnp.int32, (16, 128), 1)
    for t in range(9):
        d = 16 * t + s - c
        keep_ref[t] = jnp.where((d >= 0) & (d <= 7), 1.0, 0.0).astype(BF16)
        d = 16 * (t - 1) + s - c
        keep_ref[9 + t] = jnp.where((d >= -7) & (d <= 0), 1.0, 0.0).astype(BF16)


def build_dense(rot, keep_ref, m_ref):
    for half in range(2):
        part = rot[16 * half : 16 * half + 16]
        turned = part.astype(F32)
        turned = jnp.concatenate([turned[8:], turned[:8]], axis=0).astype(BF16)
        for j in range(2):
            lanes = slice(128 * j, 128 * j + 128)
            out_lanes = slice(256 * half + 128 * j, 256 * half + 128 * j + 128)
            for t in range(9):
                row = 16 * ((t - half + 8 * j) % 16)
                keep = keep_ref[9 * half + t]
                m_ref[row : row + 16, out_lanes] = part[:, lanes] * keep
                m_ref[256 + row : 256 + row + 16, out_lanes] = turned[:, lanes] * keep


def apply_dense(left, right, m_ref):
    new = jnp.dot(left, m_ref[:256], preferred_element_type=F32)
    return (new + jnp.dot(right, m_ref[256:], preferred_element_type=F32)).astype(BF16)


MESH = pl.DeviceIdType.MESH
CHUNKS = 8
SWAP, FIRST_X, FIRST_Y, SECOND, ALONG_Z, PLANE, FORWARD, COPIES = 0, 4, 16, 32, 38, 46, 62, 78
TOP, LOW = slice(0, 16), slice(16, 32)


def place():
    w = lax.axis_index("wide")
    n = lax.axis_index("narrow")
    z, y_lo, core = w // 4, (w // 2) % 2, w % 2
    x, y_hi = n // 2, n % 2
    return x, 2 * y_hi + y_lo, z, core


def device(x, y, z, core):
    return ((z * 2 + y % 2) * 2 + core, x * 2 + y // 2)


def seats_before(q, pairs):
    return jnp.maximum(2 * q - 2, q), 2 * q + 3 - 3 * (q // (pairs - 1))


def block(seat):
    return pl.ds(pl.multiple_of(seat * BW, BW), BW)


def main_kernel(
    pairs,
    hold,
    x_hbm,
    y_hbm,
    rot_out,
    x_ref,
    y_ref,
    mask_ref,
    g_ref,
    keep_ref,
    m_ref,
    rot_in,
    band,
    r1,
    acc1,
    ra2,
    rb2,
    acca,
    accb,
    ra3,
    rb3,
    mine,
    rz,
    load_sem,
    store_sem,
    send_sem,
    recv_sem,
):
    half = pairs // 2
    x, y, z, core = place()
    partner = device(x, y, z, 1 - core)
    along_x = [device((x + k) % 4, y, z, core) for k in range(1, 4)]
    along_y = [device(x, (y + k) % 4, z, core) for k in range(1, 4)]
    along_z = [device(x, y, (z + k) % 8, core) for k in range(1, 8)]
    width = y_ref.shape[1] // CHUNKS

    def start(copies):
        for copy in copies:
            copy.start()

    def finish(copies):
        for copy in copies:
            copy.wait()

    loads = []
    stores = []
    for k in range(CHUNKS):
        cols = slice(k * width, (k + 1) * width)
        stores.append(pltpu.make_async_copy(y_ref.at[:, cols], y_hbm.at[:, cols], store_sem.at[k]))
    for k in range(2 * pairs):
        cols = slice(k * BW, (k + 1) * BW)
        loads.append(pltpu.make_async_copy(x_hbm.at[:, cols], x_ref.at[k], load_sem.at[k]))
    start(loads)

    barrier = pltpu.get_barrier_semaphore()
    plane = [device((x + i // 4) % 4, (y + i % 4) % 4, z, core) for i in range(1, 16)]
    greeted = [partner] + plane + along_z
    for other in greeted:
        pl.semaphore_signal(barrier, inc=1, device_id=other, device_id_type=MESH)

    init_masks(mask_ref)
    init_keep(keep_ref)
    m_ref[...] = jnp.zeros_like(m_ref)
    finish(loads)

    for step in range(2):

        def remote(index, src, dst, target):
            return pltpu.make_async_remote_copy(
                src_ref=src,
                dst_ref=dst,
                send_sem=send_sem.at[step, index],
                recv_sem=recv_sem.at[step, index],
                device_id=target,
                device_id_type=MESH,
            )

        rot = rot_in if step == 0 else rot_out

        def gram_pairs(side, pieces):
            for k, (i, j) in enumerate(pieces):
                p = side * half + 4 * i + j
                if step == 0:
                    left = x_ref[hold[2 * p]]
                    right = x_ref[hold[2 * p + 1]]
                else:
                    a, b = seats_before(p, pairs)
                    left = y_ref[:, block(a)]
                    right = y_ref[:, block(b)]
                gram_band(left, right, mask_ref, g_ref.at[k], band.at[step, side, i, j])

        def ahead(base, i):
            return lax.rem(base + i + 1, 4)

        def swap(g):
            group = ahead(x, g)
            return remote(SWAP + g, band.at[step, 1 - core, group], r1.at[step, group], partner)

        def theirs(g, carry):
            gram_pairs(1 - core, [(ahead(x, g), j) for j in range(4)])
            if step == 0:

                @pl.when(g == 0)
                def _():
                    pl.semaphore_wait(barrier, len(greeted))

            swap(g).start()
            return carry

        lax.fori_loop(0, 4, theirs, 0)

        def top(g, h):
            i, j = ahead(x, g), ahead(y, h)
            return remote(
                FIRST_X + 4 * g + h, acc1.at[i, j, TOP], ra2.at[step, g, j], device(i, y, z, core)
            )

        def low(g, h):
            i, j = ahead(x, g), ahead(y, h)
            return remote(
                FIRST_Y + 4 * g + h, acc1.at[i, j, LOW], rb2.at[step, h, i], device(x, j, z, core)
            )

        def ours(g, carry):
            i = ahead(x, g)

            gram_pairs(core, [(i, ahead(y, h)) for h in range(4)])
            swap(g).wait()
            for h in range(4):
                j = ahead(y, h)
                acc1[i, j] = band[step, core, i, j] + r1[step, i, j]

                @pl.when(g < 3)
                def _():
                    top(g, h).start()

                if h < 3:
                    low(g, h).start()
            return carry

        lax.fori_loop(0, 4, ours, 0)

        def arrived(n, carry):
            a, b = n // 4, lax.rem(n, 4)
            top(a, b).wait()
            low(b, a).wait()
            return carry

        lax.fori_loop(0, 12, arrived, 0)
        acca[...] = (acc1[x, :, TOP] + ra2[step, 0]) + (ra2[step, 1] + ra2[step, 2])
        accb[...] = (acc1[:, y, LOW] + rb2[step, 0]) + (rb2[step, 1] + rb2[step, 2])

        copies = []
        for k in range(1, 4):
            copies.append(
                remote(SECOND + k, acca.at[(y + k) % 4], ra3.at[step, k - 1], along_y[k - 1])
            )
            copies.append(
                remote(SECOND + 3 + k, accb.at[(x + k) % 4], rb3.at[step, k - 1], along_x[k - 1])
            )
        start(copies)
        finish(copies)
        mine[TOP] = (acca[y] + ra3[step, 0]) + (ra3[step, 1] + ra3[step, 2])
        mine[LOW] = (accb[x] + rb3[step, 0]) + (rb3[step, 1] + rb3[step, 2])

        copies = [remote(ALONG_Z + k, mine, rz.at[step, z], along_z[k - 1]) for k in range(1, 8)]
        start(copies)
        rz[step, z] = mine[...]
        finish(copies)
        total = ((rz[step, 0] + rz[step, 1]) + (rz[step, 2] + rz[step, 3])) + (
            (rz[step, 4] + rz[step, 5]) + (rz[step, 6] + rz[step, 7])
        )

        rot[core, x, y] = rotation_band(total).astype(BF16)

        def spread_out(i):
            piece = rot.at[core, x, y]
            return remote(PLANE + i, piece, piece, device((x + i // 4) % 4, (y + i % 4) % 4, z, core))

        def source(i):
            return lax.rem(x + 4 - i // 4, 4), lax.rem(y + 4 - lax.rem(i, 4), 4)

        def arriving(i):
            sx, sy = source(i)
            piece = rot.at[core, sx, sy]
            return remote(PLANE + i, piece, piece, partner)

        def forward(i):
            sx, sy = source(i)
            piece = rot.at[core, sx, sy]
            return remote(FORWARD + i, piece, piece, partner)

        def forwarded(i):
            sx, sy = source(i)
            piece = rot.at[1 - core, sx, sy]
            return remote(FORWARD + i, piece, piece, partner)

        for i in range(1, 16):
            spread_out(i).start()
        forward(0).start()

        def apply_pair(side, i, k):
            sx, sy = source(i)
            p = side * half + 4 * sx + sy
            build_dense(rot[side, sx, sy], keep_ref, m_ref.at[k])
            left = x_ref[hold[2 * p]]
            right = x_ref[hold[2 * p + 1]]
            cols = pl.ds(pl.multiple_of(p * 2 * BW, 2 * BW), 2 * BW)
            y_ref[:, cols] = apply_dense(left, right, m_ref.at[k])

        def first_half(h, carry):
            for k in range(4):
                i = 4 * h + k

                @pl.when(i > 0)
                def _():
                    arriving(i).wait_recv()
                    forward(i).start()

            if step == 0:
                for k in range(4):
                    apply_pair(core, 4 * h + k, k)
            return carry

        def second_half(h, carry):
            for k in range(4):
                forwarded(4 * h + k).wait_recv()
            if step == 0:
                for k in range(4):
                    apply_pair(1 - core, 4 * h + k, k)
            return carry

        lax.fori_loop(0, 4, first_half, 0)
        lax.fori_loop(0, 4, second_half, 0)
        for i in range(1, 16):
            spread_out(i).wait_send()
        for i in range(16):
            forward(i).wait_send()
        if step == 0:
            start(stores)
    finish(stores)


def main_call(x, holders, pairs):
    rows, cols = x.shape
    vmem = pl.BlockSpec(memory_space=pltpu.VMEM)
    hbm = pl.BlockSpec(memory_space=pl.ANY)
    out, rot = pl.pallas_call(
        functools.partial(main_kernel, pairs),
        out_shape=(
            jax.ShapeDtypeStruct((rows, cols), BF16),
            jax.ShapeDtypeStruct((2, 4, 4, 32, BW), BF16),
        ),
        in_specs=[pl.BlockSpec(memory_space=pltpu.SMEM), hbm],
        out_specs=(hbm, vmem),
        scratch_shapes=[
            pltpu.VMEM((2 * pairs, rows, BW), BF16),
            pltpu.VMEM((rows, cols), BF16),
            pltpu.VMEM((35, 8, 128), F32),
            pltpu.VMEM((4, 3, BW, BW), F32),
            pltpu.VMEM((18, 16, 128), BF16),
            pltpu.VMEM((4, 2 * BW, 2 * BW), BF16),
            pltpu.VMEM((2, 4, 4, 32, BW), BF16),
            pltpu.VMEM((2, 2, 4, 4, 32, BW), F32),
            pltpu.VMEM((2, 4, 4, 32, BW), F32),
            pltpu.VMEM((4, 4, 32, BW), F32),
            pltpu.VMEM((2, 3, 4, 16, BW), F32),
            pltpu.VMEM((2, 3, 4, 16, BW), F32),
            pltpu.VMEM((4, 16, BW), F32),
            pltpu.VMEM((4, 16, BW), F32),
            pltpu.VMEM((2, 3, 16, BW), F32),
            pltpu.VMEM((2, 3, 16, BW), F32),
            pltpu.VMEM((32, BW), F32),
            pltpu.VMEM((2, 8, 32, BW), F32),
            pltpu.SemaphoreType.DMA((2 * pairs,)),
            pltpu.SemaphoreType.DMA((CHUNKS,)),
            pltpu.SemaphoreType.DMA((2, COPIES)),
            pltpu.SemaphoreType.DMA((2, COPIES)),
        ],
        compiler_params=pltpu.CompilerParams(collective_id=0, has_side_effects=True),
    )(holders, x)
    return out, rot.reshape(pairs, 32, BW)


def last_kernel(
    pairs, hold, y_hbm, rot, out_hbm, y_ref, keep_ref, m_ref, z_ref, load_sem, store_sem
):
    width = y_ref.shape[1] // CHUNKS
    per_chunk = pairs // CHUNKS

    def load(k):
        cols = pl.ds(pl.multiple_of(k * width, width), width)
        return pltpu.make_async_copy(y_hbm.at[:, cols], y_ref.at[:, cols], load_sem.at[k])

    def store(seat, before):
        return pltpu.make_async_copy(
            z_ref.at[:, block(seat)], out_hbm.at[:, block(hold[before])], store_sem.at[seat]
        )

    for k in range(CHUNKS):
        load(k).start()
    init_keep(keep_ref)
    m_ref[...] = jnp.zeros_like(m_ref)
    load(0).wait()

    def body(i, carry):
        @pl.when(i + 1 < CHUNKS)
        def _():
            load(i + 1).wait()

        def inner(h, carry):
            for k in range(4):
                q = i * per_chunk + 4 * h + k
                build_dense(rot[q], keep_ref, m_ref.at[k])
                a, b = seats_before(q, pairs)
                cols = pl.ds(pl.multiple_of(q * 2 * BW, 2 * BW), 2 * BW)
                z_ref[:, cols] = apply_dense(y_ref[:, block(a)], y_ref[:, block(b)], m_ref.at[k])
                store(2 * q, a).start()
                store(2 * q + 1, b).start()
            return carry

        return lax.fori_loop(0, per_chunk // 4, inner, carry)

    lax.fori_loop(0, CHUNKS, body, 0)

    def drain(q, carry):
        a, b = seats_before(q, pairs)
        store(2 * q, a).wait()
        store(2 * q + 1, b).wait()
        return carry

    lax.fori_loop(0, pairs, drain, 0)


def last_call(y, holders, rot, pairs):
    rows, cols = y.shape
    vmem = pl.BlockSpec(memory_space=pltpu.VMEM)
    hbm = pl.BlockSpec(memory_space=pl.ANY)
    return pl.pallas_call(
        functools.partial(last_kernel, pairs),
        out_shape=jax.ShapeDtypeStruct((rows, cols), BF16),
        in_specs=[pl.BlockSpec(memory_space=pltpu.SMEM), hbm, vmem],
        out_specs=hbm,
        scratch_shapes=[
            pltpu.VMEM((rows, cols), BF16),
            pltpu.VMEM((18, 16, 128), BF16),
            pltpu.VMEM((4, 2 * BW, 2 * BW), BF16),
            pltpu.VMEM((rows, cols), BF16),
            pltpu.SemaphoreType.DMA((CHUNKS,)),
            pltpu.SemaphoreType.DMA((2 * pairs,)),
        ],
    )(holders, y, rot)


def per_device(gradient, seating):
    slots = gradient.shape[1] // BW
    pairs = slots // 2
    seat_of = seating.astype(jnp.int32)
    holders = occupants(seat_of, slots)
    moved, rot = main_call(gradient, holders, pairs)
    return last_call(moved, holders, rot, pairs)


def solution(mesh):
    in_specs = (P(("wide", "narrow"), None), P())
    out_specs = P(("wide", "narrow"), None)
    return jax.shard_map(
        per_device, mesh=mesh, in_specs=in_specs, out_specs=out_specs, check_vma=False
    )
```

```python
import functools

import jax
import jax.numpy as jnp
from jax import lax
from jax.experimental import pallas as pl
from jax.experimental.pallas import tpu as pltpu
from jax.sharding import PartitionSpec as P

ROUNDS = 8
BW = 256
F32 = jnp.float32
BF16 = jnp.bfloat16


def occupants(seat_of, total_slots):
    block_ids = jnp.arange(total_slots, dtype=jnp.int32)
    matches = seat_of[None, :] == block_ids[:, None]
    return jnp.sum(jnp.where(matches, block_ids[None, :], 0), axis=1).astype(jnp.int32)


def init_masks(mask_ref):
    s = lax.broadcasted_iota(jnp.int32, (8, 128), 0)
    c = lax.broadcasted_iota(jnp.int32, (8, 128), 1)
    for t in range(-1, 17):
        d = 8 * t + s - c
        mask_ref[t + 1] = jnp.where((d >= -7) & (d <= 7), 1.0, 0.0).astype(F32)
    for t in range(17):
        d = 8 * t + s - c
        mask_ref[18 + t] = jnp.where((d >= 0) & (d <= 7), 1.0, 0.0).astype(F32)


def dot_t(a, b):
    return lax.dot_general(a, b, (((0,), (0,)), ((), ())), preferred_element_type=F32)


def gram_band(left, right, mask_ref, g_ref, out_ref):
    g_ref[0] = dot_t(left, right)
    g_ref[1] = dot_t(left, left)
    g_ref[2] = dot_t(right, right)
    for j in range(2):
        lanes = slice(128 * j, 128 * j + 128)
        acc = [jnp.zeros((8, 128), F32) for _ in range(4)]
        for t in range(-1, 17):
            u = (16 * j + t) % 32
            acc[u % 2] += g_ref[0, 8 * u : 8 * u + 8, lanes] * mask_ref[t + 1]
        for t in range(17):
            u = (16 * j + t) % 32
            mask = mask_ref[18 + t]
            acc[2 + u % 2] += g_ref[1, 8 * u : 8 * u + 8, lanes] * mask
            acc[2 + (u + 1) % 2] += g_ref[2, 8 * u : 8 * u + 8, lanes] * mask
        for r in range(4):
            out_ref[8 * r : 8 * r + 8, lanes] = acc[r]


def lane_roll(x, back):
    return pltpu.roll(x, (-back) % x.shape[1], 1)


def row_roll(x, down):
    return pltpu.roll(x, down % x.shape[0], 0)


def iota(shape, axis):
    return lax.broadcasted_iota(jnp.int32, shape, axis)


def skew(x, sign):
    c = iota(x.shape, 1)
    for b in (1, 2, 4, 8):
        x = jnp.where((c & b) != 0, row_roll(x, sign * b), x)
    return x


def spread(x):
    y = jnp.broadcast_to(x, (8, x.shape[1]))
    d = iota(y.shape, 0)
    for b in (1, 2, 4):
        y = jnp.where((d & b) != 0, lane_roll(y, b), y)
    return y


def rotation_band(band):
    cross = skew(band[:16], -1)
    own = skew(band[16:], -1)
    lr = cross[:8]
    ll = own[:8]
    rr = own[8:]
    d = iota((8, BW), 0)
    flipped = [lr[0:1]] + [lane_roll(cross[16 - k : 17 - k], k) for k in range(1, 8)]
    rl = jnp.concatenate(flipped, axis=0)
    ca = jnp.where(d == 0, 1.0, 0.0).astype(F32)
    cb = jnp.zeros((8, BW), F32)
    cc = jnp.zeros((8, BW), F32)
    cd = ca
    for r in range(ROUNDS):
        a = ll[0:1]
        c = rr[0:1]
        off = lr[0:1]
        spread_ac = c - a
        damp = (a + c) / 16.0 + 1e-06
        radius = jnp.sqrt(spread_ac * spread_ac + 4.0 * off * off + damp * damp)
        tangent = 2.0 * off / (spread_ac + radius)
        cs = 1.0 / jnp.sqrt(1.0 + tangent * tangent)
        sn = tangent * cs
        if r < ROUNDS - 1:
            csd = spread(cs)
            snd = spread(sn)
            ll1 = ll * cs - lr * sn
            lr1 = ll * sn + lr * cs
            rl1 = rl * cs - rr * sn
            rr1 = rl * sn + rr * cs
            ll = csd * ll1 - snd * rl1
            rl = snd * ll1 + csd * rl1
            lr = csd * lr1 - snd * rr1
            rr = snd * lr1 + csd * rr1
        ca, cc = cs * ca - sn * cc, sn * ca + cs * cc
        cb, cd = cs * cb - sn * cd, sn * cb + cs * cd
        if r < ROUNDS - 1:
            lr = jnp.where(d == 0, row_roll(rl, -1), row_roll(lane_roll(lr, 1), 1))
            rl = jnp.where(d == 7, 0.0, row_roll(rl, -1))
            rr = lane_roll(rr, 1)
            cc = jnp.where(d == 0, 0.0, row_roll(lane_roll(cc, 1), 1))
            cd = jnp.where(d == 0, 0.0, row_roll(lane_roll(cd, 1), 1))
    first = jnp.concatenate([ca, cb], axis=0)
    second = row_roll(jnp.concatenate([lane_roll(cd, -7), lane_roll(cc, -7)], axis=0), 1)
    return jnp.concatenate([skew(first, 1), skew(second, 1)], axis=0)


def init_keep(keep_ref):
    s = lax.broadcasted_iota(jnp.int32, (16, 128), 0)
    c = lax.broadcasted_iota(jnp.int32, (16, 128), 1)
    for t in range(9):
        d = 16 * t + s - c
        keep_ref[t] = jnp.where((d >= 0) & (d <= 7), 1.0, 0.0).astype(BF16)
        d = 16 * (t - 1) + s - c
        keep_ref[9 + t] = jnp.where((d >= -7) & (d <= 0), 1.0, 0.0).astype(BF16)


def build_dense(rot, keep_ref, m_ref):
    for half in range(2):
        part = rot[16 * half : 16 * half + 16]
        turned = part.astype(F32)
        turned = jnp.concatenate([turned[8:], turned[:8]], axis=0).astype(BF16)
        for j in range(2):
            lanes = slice(128 * j, 128 * j + 128)
            out_lanes = slice(256 * half + 128 * j, 256 * half + 128 * j + 128)
            for t in range(9):
                row = 16 * ((t - half + 8 * j) % 16)
                keep = keep_ref[9 * half + t]
                m_ref[row : row + 16, out_lanes] = part[:, lanes] * keep
                m_ref[256 + row : 256 + row + 16, out_lanes] = turned[:, lanes] * keep


def apply_dense(left, right, m_ref):
    new = jnp.dot(left, m_ref[:256], preferred_element_type=F32)
    return (new + jnp.dot(right, m_ref[256:], preferred_element_type=F32)).astype(BF16)


MESH = pl.DeviceIdType.MESH
CHUNKS = 8
SWAP, FIRST_X, FIRST_Y, SECOND, ALONG_Z, PLANE, FORWARD, COPIES = 0, 4, 16, 32, 38, 46, 62, 78
TOP, LOW = slice(0, 16), slice(16, 32)


def place():
    w = lax.axis_index("wide")
    n = lax.axis_index("narrow")
    z, y_lo, core = w // 4, (w // 2) % 2, w % 2
    x, y_hi = n // 2, n % 2
    return x, 2 * y_hi + y_lo, z, core


def device(x, y, z, core):
    return ((z * 2 + y % 2) * 2 + core, x * 2 + y // 2)


def seats_before(q, pairs):
    return jnp.maximum(2 * q - 2, q), 2 * q + 3 - 3 * (q // (pairs - 1))


def block(seat):
    return pl.ds(pl.multiple_of(seat * BW, BW), BW)


def main_kernel(
    pairs,
    hold,
    x_hbm,
    y_hbm,
    rot_out,
    x_ref,
    y_ref,
    mask_ref,
    g_ref,
    keep_ref,
    m_ref,
    rot_in,
    band,
    r1,
    acc1,
    ra2,
    rb2,
    acca,
    accb,
    ra3,
    rb3,
    mine,
    rz,
    load_sem,
    store_sem,
    send_sem,
    recv_sem,
):
    half = pairs // 2
    x, y, z, core = place()
    partner = device(x, y, z, 1 - core)
    along_x = [device((x + k) % 4, y, z, core) for k in range(1, 4)]
    along_y = [device(x, (y + k) % 4, z, core) for k in range(1, 4)]
    along_z = [device(x, y, (z + k) % 8, core) for k in range(1, 8)]
    width = y_ref.shape[1] // CHUNKS

    def start(copies):
        for copy in copies:
            copy.start()

    def finish(copies):
        for copy in copies:
            copy.wait()

    loads = []
    stores = []
    for k in range(CHUNKS):
        cols = slice(k * width, (k + 1) * width)
        stores.append(pltpu.make_async_copy(y_ref.at[:, cols], y_hbm.at[:, cols], store_sem.at[k]))
    for k in range(2 * pairs):
        cols = slice(k * BW, (k + 1) * BW)
        loads.append(pltpu.make_async_copy(x_hbm.at[:, cols], x_ref.at[k], load_sem.at[k]))
    start(loads)

    barrier = pltpu.get_barrier_semaphore()
    plane = [device((x + i // 4) % 4, (y + i % 4) % 4, z, core) for i in range(1, 16)]
    greeted = [partner] + plane + along_z
    for other in greeted:
        pl.semaphore_signal(barrier, inc=1, device_id=other, device_id_type=MESH)

    init_masks(mask_ref)
    init_keep(keep_ref)
    m_ref[...] = jnp.zeros_like(m_ref)
    finish(loads)

    for step in range(2):

        def remote(index, src, dst, target):
            return pltpu.make_async_remote_copy(
                src_ref=src,
                dst_ref=dst,
                send_sem=send_sem.at[step, index],
                recv_sem=recv_sem.at[step, index],
                device_id=target,
                device_id_type=MESH,
            )

        rot = rot_in if step == 0 else rot_out

        def gram_pairs(side, pieces):
            for k, (i, j) in enumerate(pieces):
                p = side * half + 4 * i + j
                if step == 0:
                    left = x_ref[hold[2 * p]]
                    right = x_ref[hold[2 * p + 1]]
                else:
                    a, b = seats_before(p, pairs)
                    left = y_ref[:, block(a)]
                    right = y_ref[:, block(b)]
                gram_band(left, right, mask_ref, g_ref.at[k], band.at[step, side, i, j])

        def ahead(base, i):
            return lax.rem(base + i + 1, 4)

        def swap(g):
            group = ahead(x, g)
            return remote(SWAP + g, band.at[step, 1 - core, group], r1.at[step, group], partner)

        def theirs(g, carry):
            gram_pairs(1 - core, [(ahead(x, 2 * g + k), j) for k in range(2) for j in range(4)])
            if step == 0:

                @pl.when(g == 0)
                def _():
                    pl.semaphore_wait(barrier, len(greeted))

            swap(2 * g).start()
            swap(2 * g + 1).start()
            return carry

        lax.fori_loop(0, 2, theirs, 0)

        def top(g, h):
            i, j = ahead(x, g), ahead(y, h)
            return remote(
                FIRST_X + 4 * g + h, acc1.at[i, j, TOP], ra2.at[step, g, j], device(i, y, z, core)
            )

        def low(g, h):
            i, j = ahead(x, g), ahead(y, h)
            return remote(
                FIRST_Y + 4 * g + h, acc1.at[i, j, LOW], rb2.at[step, h, i], device(x, j, z, core)
            )

        def ours(g, carry):
            i = ahead(x, g)

            gram_pairs(core, [(i, ahead(y, h)) for h in range(4)])
            swap(g).wait()
            for h in range(4):
                j = ahead(y, h)
                acc1[i, j] = band[step, core, i, j] + r1[step, i, j]

                @pl.when(g < 3)
                def _():
                    top(g, h).start()

                if h < 3:
                    low(g, h).start()
            return carry

        lax.fori_loop(0, 4, ours, 0)

        def arrived(n, carry):
            a, b = n // 4, lax.rem(n, 4)
            top(a, b).wait()
            low(b, a).wait()
            return carry

        lax.fori_loop(0, 12, arrived, 0)
        acca[...] = (acc1[x, :, TOP] + ra2[step, 0]) + (ra2[step, 1] + ra2[step, 2])
        accb[...] = (acc1[:, y, LOW] + rb2[step, 0]) + (rb2[step, 1] + rb2[step, 2])

        copies = []
        for k in range(1, 4):
            copies.append(
                remote(SECOND + k, acca.at[(y + k) % 4], ra3.at[step, k - 1], along_y[k - 1])
            )
            copies.append(
                remote(SECOND + 3 + k, accb.at[(x + k) % 4], rb3.at[step, k - 1], along_x[k - 1])
            )
        start(copies)
        finish(copies)
        mine[TOP] = (acca[y] + ra3[step, 0]) + (ra3[step, 1] + ra3[step, 2])
        mine[LOW] = (accb[x] + rb3[step, 0]) + (rb3[step, 1] + rb3[step, 2])

        copies = [remote(ALONG_Z + k, mine, rz.at[step, z], along_z[k - 1]) for k in range(1, 8)]
        start(copies)
        rz[step, z] = mine[...]
        finish(copies)
        total = ((rz[step, 0] + rz[step, 1]) + (rz[step, 2] + rz[step, 3])) + (
            (rz[step, 4] + rz[step, 5]) + (rz[step, 6] + rz[step, 7])
        )

        rot[core, x, y] = rotation_band(total).astype(BF16)

        def spread_out(i):
            piece = rot.at[core, x, y]
            return remote(PLANE + i, piece, piece, device((x + i // 4) % 4, (y + i % 4) % 4, z, core))

        def source(i):
            return lax.rem(x + 4 - i // 4, 4), lax.rem(y + 4 - lax.rem(i, 4), 4)

        def arriving(i):
            sx, sy = source(i)
            piece = rot.at[core, sx, sy]
            return remote(PLANE + i, piece, piece, partner)

        def forward(i):
            sx, sy = source(i)
            piece = rot.at[core, sx, sy]
            return remote(FORWARD + i, piece, piece, partner)

        def forwarded(i):
            sx, sy = source(i)
            piece = rot.at[1 - core, sx, sy]
            return remote(FORWARD + i, piece, piece, partner)

        for i in range(1, 16):
            spread_out(i).start()
        forward(0).start()

        def apply_pair(side, i, k):
            sx, sy = source(i)
            p = side * half + 4 * sx + sy
            build_dense(rot[side, sx, sy], keep_ref, m_ref.at[k])
            left = x_ref[hold[2 * p]]
            right = x_ref[hold[2 * p + 1]]
            cols = pl.ds(pl.multiple_of(p * 2 * BW, 2 * BW), 2 * BW)
            y_ref[:, cols] = apply_dense(left, right, m_ref.at[k])

        def first_half(h, carry):
            for k in range(4):
                i = 4 * h + k

                @pl.when(i > 0)
                def _():
                    arriving(i).wait_recv()
                    forward(i).start()

            if step == 0:
                for k in range(4):
                    apply_pair(core, 4 * h + k, k)
            return carry

        def second_half(h, carry):
            for k in range(4):
                forwarded(4 * h + k).wait_recv()
            if step == 0:
                for k in range(4):
                    apply_pair(1 - core, 4 * h + k, k)
            return carry

        lax.fori_loop(0, 4, first_half, 0)
        lax.fori_loop(0, 4, second_half, 0)
        for i in range(1, 16):
            spread_out(i).wait_send()
        for i in range(16):
            forward(i).wait_send()
        if step == 0:
            start(stores)
    finish(stores)


def main_call(x, holders, pairs):
    rows, cols = x.shape
    vmem = pl.BlockSpec(memory_space=pltpu.VMEM)
    hbm = pl.BlockSpec(memory_space=pl.ANY)
    out, rot = pl.pallas_call(
        functools.partial(main_kernel, pairs),
        out_shape=(
            jax.ShapeDtypeStruct((rows, cols), BF16),
            jax.ShapeDtypeStruct((2, 4, 4, 32, BW), BF16),
        ),
        in_specs=[pl.BlockSpec(memory_space=pltpu.SMEM), hbm],
        out_specs=(hbm, vmem),
        scratch_shapes=[
            pltpu.VMEM((2 * pairs, rows, BW), BF16),
            pltpu.VMEM((rows, cols), BF16),
            pltpu.VMEM((35, 8, 128), F32),
            pltpu.VMEM((8, 3, BW, BW), F32),
            pltpu.VMEM((18, 16, 128), BF16),
            pltpu.VMEM((4, 2 * BW, 2 * BW), BF16),
            pltpu.VMEM((2, 4, 4, 32, BW), BF16),
            pltpu.VMEM((2, 2, 4, 4, 32, BW), F32),
            pltpu.VMEM((2, 4, 4, 32, BW), F32),
            pltpu.VMEM((4, 4, 32, BW), F32),
            pltpu.VMEM((2, 3, 4, 16, BW), F32),
            pltpu.VMEM((2, 3, 4, 16, BW), F32),
            pltpu.VMEM((4, 16, BW), F32),
            pltpu.VMEM((4, 16, BW), F32),
            pltpu.VMEM((2, 3, 16, BW), F32),
            pltpu.VMEM((2, 3, 16, BW), F32),
            pltpu.VMEM((32, BW), F32),
            pltpu.VMEM((2, 8, 32, BW), F32),
            pltpu.SemaphoreType.DMA((2 * pairs,)),
            pltpu.SemaphoreType.DMA((CHUNKS,)),
            pltpu.SemaphoreType.DMA((2, COPIES)),
            pltpu.SemaphoreType.DMA((2, COPIES)),
        ],
        compiler_params=pltpu.CompilerParams(collective_id=0, has_side_effects=True),
    )(holders, x)
    return out, rot.reshape(pairs, 32, BW)


def last_kernel(
    pairs, hold, y_hbm, rot, out_hbm, y_ref, keep_ref, m_ref, z_ref, load_sem, store_sem
):
    width = y_ref.shape[1] // CHUNKS
    per_chunk = pairs // CHUNKS

    def load(k):
        cols = pl.ds(pl.multiple_of(k * width, width), width)
        return pltpu.make_async_copy(y_hbm.at[:, cols], y_ref.at[:, cols], load_sem.at[k])

    def store(seat, before):
        return pltpu.make_async_copy(
            z_ref.at[:, block(seat)], out_hbm.at[:, block(hold[before])], store_sem.at[seat]
        )

    for k in range(CHUNKS):
        load(k).start()
    init_keep(keep_ref)
    m_ref[...] = jnp.zeros_like(m_ref)
    load(0).wait()

    def body(i, carry):
        @pl.when(i + 1 < CHUNKS)
        def _():
            load(i + 1).wait()

        def inner(h, carry):
            for k in range(4):
                q = i * per_chunk + 4 * h + k
                build_dense(rot[q], keep_ref, m_ref.at[k])
                a, b = seats_before(q, pairs)
                cols = pl.ds(pl.multiple_of(q * 2 * BW, 2 * BW), 2 * BW)
                z_ref[:, cols] = apply_dense(y_ref[:, block(a)], y_ref[:, block(b)], m_ref.at[k])
                store(2 * q, a).start()
                store(2 * q + 1, b).start()
            return carry

        return lax.fori_loop(0, per_chunk // 4, inner, carry)

    lax.fori_loop(0, CHUNKS, body, 0)

    def drain(q, carry):
        a, b = seats_before(q, pairs)
        store(2 * q, a).wait()
        store(2 * q + 1, b).wait()
        return carry

    lax.fori_loop(0, pairs, drain, 0)


def last_call(y, holders, rot, pairs):
    rows, cols = y.shape
    vmem = pl.BlockSpec(memory_space=pltpu.VMEM)
    hbm = pl.BlockSpec(memory_space=pl.ANY)
    return pl.pallas_call(
        functools.partial(last_kernel, pairs),
        out_shape=jax.ShapeDtypeStruct((rows, cols), BF16),
        in_specs=[pl.BlockSpec(memory_space=pltpu.SMEM), hbm, vmem],
        out_specs=hbm,
        scratch_shapes=[
            pltpu.VMEM((rows, cols), BF16),
            pltpu.VMEM((18, 16, 128), BF16),
            pltpu.VMEM((4, 2 * BW, 2 * BW), BF16),
            pltpu.VMEM((rows, cols), BF16),
            pltpu.SemaphoreType.DMA((CHUNKS,)),
            pltpu.SemaphoreType.DMA((2 * pairs,)),
        ],
    )(holders, y, rot)


def per_device(gradient, seating):
    slots = gradient.shape[1] // BW
    pairs = slots // 2
    seat_of = seating.astype(jnp.int32)
    holders = occupants(seat_of, slots)
    moved, rot = main_call(gradient, holders, pairs)
    return last_call(moved, holders, rot, pairs)


def solution(mesh):
    in_specs = (P(("wide", "narrow"), None), P())
    out_specs = P(("wide", "narrow"), None)
    return jax.shard_map(
        per_device, mesh=mesh, in_specs=in_specs, out_specs=out_specs, check_vma=False
    )
```
